256 devices in a mesh: dp: 32 (over z_hi, x, core), ctx: 8 (over y, z_lo).
Axes of the slice: x: 4, y: 4, z: 8 (z_hi: 4, z_lo: 2; z = z_hi * 2 + z_lo), core: 2. Of those that a mesh axis runs over, the one named last changes fastest.
Arguments:
- clip_in: bfloat16 [32, 32, 4, 96, 128], P('dp', 'ctx'), may hold values from -100 to 100
- norm_gain: float32 [128], replicated, may hold values from 0.1 to 1.9
- norm_bias: float32 [128], replicated, may hold values from -3 to 3
- conv_weight: bfloat16 [3456, 256], replicated, may hold values from -0.109375 to 0.109375
- short_weight: bfloat16 [128, 256], replicated, may hold values from -0.5 to 0.5
- out_cotangent: bfloat16 [32, 32, 4, 96, 256], P('dp', 'ctx'), may hold values from -6 to 6
Outputs:
- clip_out: bfloat16 [32, 32, 4, 96, 256], P('dp', 'ctx')
- clip_grad: bfloat16 [32, 32, 4, 96, 128], P('dp', 'ctx')
- conv_grad: float32 [3456, 256], P('dp', 'ctx')
- short_grad: float32 [128, 256], P('dp', 'ctx')
The draws below stay inside these ranges and needn't reach their ends.
All inputs are finite; a program needn't handle non-finite values.
Results may differ from the reference program's by a relative error of at most 0.0027.
Values may be sent and summed in bfloat16 or wider, within the bound.
A program may use at most 128 MiB of HBM per device.

```python
import math
import jax
import jax.numpy as jnp
from jax import lax

CIN = 128
COUT = 256
GROUPS = 32
KT = 3
KS = 3
ROWS = 4
COLS = 96
CLIPS = 32
FRAMES = 32


def draw_clip_in(key, part):
    key_base, key_chan, key_rows, key_offset = jax.random.split(key, 4)
    extent = (CLIPS, FRAMES, ROWS, COLS, CIN)
    channel_scale = jnp.exp(jax.random.uniform(key_chan, (CIN,), jnp.float32, math.log(0.3), math.log(3.0)))
    row_scale = jnp.exp(jax.random.uniform(key_rows, (CLIPS, FRAMES, ROWS, 1, 1), jnp.float32, math.log(0.5), math.log(2.0)))
    frame_ramp = jnp.exp(math.log(3.0) * jnp.arange(FRAMES, dtype=jnp.float32) / max(FRAMES - 1, 1)).reshape(1, FRAMES, 1, 1, 1)
    base_vals = jnp.clip(jax.random.normal(key_base, extent, jnp.float32), -4.0, 4.0)
    offset_vals = 0.3 * jnp.clip(jax.random.normal(key_offset, (CLIPS, 1, 1, 1, CIN), jnp.float32), -3.0, 3.0)
    return ((base_vals * channel_scale + offset_vals) * row_scale * frame_ramp).astype(jnp.bfloat16)


def with_spikes(entries, stream_key, source, target, parts, factor):
    def block_of(axis_at):
        return (jnp.arange(entries.shape[axis_at]) // (entries.shape[axis_at] // parts)).reshape((-1,) + (1,) * (entries.ndim - 1 - axis_at))

    near = jax.random.permutation(stream_key, parts)[block_of(target)]
    other_side = (block_of(target) + parts // 2) % parts
    return jnp.where((block_of(source) == near) | (block_of(source) == other_side), factor * entries, entries)


def block_scale(rng, dims, cuts, low, high):
    gain, own = 1.0, jax.random.fold_in(rng, 6)
    for axis_at, parts in cuts:
        heights = jnp.exp(jax.random.uniform(jax.random.fold_in(own, axis_at), (parts,), jnp.float32, low / len(cuts), high / len(cuts)))
        gain = gain * jnp.repeat(heights, dims[axis_at] // parts).reshape([-1 if axis == axis_at else 1 for axis in range(len(dims))])
    return gain


def normal_values(own_key, shape, deviation, bound, shards=(), held_as=jnp.bfloat16):
    values = jax.random.normal(own_key, shape, jnp.float32) * deviation
    if len(shards) > 0:
        values = block_scale(own_key, shape, shards, -0.22, 0.18) * values
    return jnp.clip(values, min=-bound, max=bound).astype(held_as)


def gaussian_with(stream_key, shape, width, bound, cuts, heavy, kind=jnp.bfloat16):
    values = width * jax.random.normal(stream_key, shape, jnp.float32)
    if cuts:
        values = values * block_scale(stream_key, shape, cuts, -0.22, 0.18)
    return jnp.clip(with_spikes(values, jax.random.fold_in(stream_key, 3), *heavy), -bound, bound).astype(kind)


def setup_inputs(seed: int = 0) -> dict:
    arg_keys = jax.random.split(jax.random.key(seed), 7)
    clip_in = draw_clip_in(jax.random.fold_in(arg_keys[6], 71), 0)
    norm_gain = jnp.clip(1.0 + 0.18 * jax.random.normal(arg_keys[1], (CIN,), jnp.float32), 0.1, 1.9)
    norm_bias = normal_values(arg_keys[2], (CIN,), 0.5, 3.0, (), jnp.float32)
    conv_weight = normal_values(arg_keys[3], (KT * KS * KS * CIN, COUT), (KT * KS * KS * CIN) ** -0.5, 0.109375)
    short_weight = normal_values(arg_keys[4], (CIN, COUT), CIN ** -0.5, 0.5)
    out_cotangent = gaussian_with(arg_keys[5], (CLIPS, FRAMES, ROWS, COLS, COUT), 1.0, 6.0, ((0, 32), (1, 8)), (0, 4, 32, 2.75))
    return {"clip_in": clip_in, "norm_gain": norm_gain, "norm_bias": norm_bias, "conv_weight": conv_weight, "short_weight": short_weight, "out_cotangent": out_cotangent}


epsilon = 1e-06

def reference(clip_in, norm_gain, norm_bias, conv_weight, short_weight, out_cotangent):
    per_group = CIN // GROUPS
    members = FRAMES * ROWS * COLS * per_group
    w_back = conv_weight.reshape(KT, KS * KS, CIN, COUT).transpose(0, 1, 3, 2).reshape(KT, KS * KS * COUT, CIN)

    def one_clip(inputs):
        clip_vals, clip_cot = inputs
        widened = clip_vals.astype(jnp.float32)
        grouped = widened.reshape(FRAMES, ROWS, COLS, GROUPS, per_group)
        group_mean = lax.optimization_barrier(jnp.sum(grouped, axis=(0, 1, 2, 4))) / members
        variance = lax.optimization_barrier(jnp.sum(grouped * grouped, axis=(0, 1, 2, 4))) / members - group_mean * group_mean
        inv_std = lax.rsqrt(variance + epsilon)
        mean_chan = jnp.repeat(group_mean, per_group)
        inv_chan = jnp.repeat(inv_std, per_group)
        standard = (widened - mean_chan) * inv_chan
        affine = standard * norm_gain + norm_bias
        hidden = jax.nn.silu(affine).astype(jnp.bfloat16)
        padded = jnp.concatenate([hidden[:1], hidden[:1], hidden], axis=0)
        padded = jnp.pad(padded, ((0, 0), (1, 1), (1, 1), (0, 0)))
        pieces = []
        for tap_t in range(KT):
            for tap_r in range(KS):
                for tap_c in range(KS):
                    pieces.append(padded[tap_t:tap_t + FRAMES, tap_r:tap_r + ROWS, tap_c:tap_c + COLS])
        columns = jnp.concatenate(pieces, axis=-1).reshape(-1, KT * KS * KS * CIN)
        cot_flat = clip_cot.reshape(-1, COUT)
        in_flat = clip_vals.reshape(-1, CIN)
        result = jnp.dot(columns, conv_weight, preferred_element_type=jnp.float32)
        result = result + jnp.dot(in_flat, short_weight, preferred_element_type=jnp.float32)
        result = result.astype(jnp.bfloat16).reshape(FRAMES, ROWS, COLS, COUT)
        conv_part = lax.dot_general(columns, cot_flat, (((0,), (0,)), ((), ())), preferred_element_type=jnp.float32)
        short_part = lax.dot_general(in_flat, cot_flat, (((0,), (0,)), ((), ())), preferred_element_type=jnp.float32)
        padded_cot = jnp.pad(clip_cot, ((2, 2), (1, 1), (1, 1), (0, 0)))
        spatial = []
        for tap_r in range(KS):
            for tap_c in range(KS):
                spatial.append(padded_cot[:, 2 - tap_r:2 - tap_r + ROWS, 2 - tap_c:2 - tap_c + COLS])
        spatial = jnp.concatenate(spatial, axis=-1)
        back_all = jnp.zeros(((FRAMES + 2) * ROWS * COLS, CIN), jnp.float32)
        for tap_t in range(KT):
            block = spatial[2 - tap_t:2 - tap_t + FRAMES + 2].reshape(-1, KS * KS * COUT)
            back_all = back_all + jnp.dot(block, w_back[tap_t], preferred_element_type=jnp.float32)
        back_all = back_all.reshape(FRAMES + 2, ROWS, COLS, CIN)
        grad_hidden = back_all[2:]
        grad_hidden = grad_hidden.at[0].add(back_all[0] + back_all[1])
        logistic = jax.nn.sigmoid(affine)
        grad_standard = grad_hidden * logistic * (1.0 + affine * (1.0 - logistic)) * norm_gain
        grouped_grad = grad_standard.reshape(FRAMES, ROWS, COLS, GROUPS, per_group)
        grouped_std = standard.reshape(FRAMES, ROWS, COLS, GROUPS, per_group)
        mean_grad = jnp.repeat(lax.optimization_barrier(jnp.sum(grouped_grad, axis=(0, 1, 2, 4))) / members, per_group)
        mean_cross = jnp.repeat(lax.optimization_barrier(jnp.sum(grouped_grad * grouped_std, axis=(0, 1, 2, 4))) / members, per_group)
        shortcut = lax.dot_general(cot_flat, short_weight, (((1,), (1,)), ((), ())), preferred_element_type=jnp.float32)
        in_grad = (grad_standard - mean_grad - standard * mean_cross) * inv_chan + shortcut.reshape(FRAMES, ROWS, COLS, CIN)
        return (result, in_grad.astype(jnp.bfloat16), conv_part, short_part)
    clip_out, clip_grad, conv_parts, short_parts = lax.map(one_clip, (clip_in, out_cotangent))
    scale_factor = 1.0 / (CLIPS * FRAMES)
    conv_grad = lax.optimization_barrier(jnp.sum(conv_parts, axis=0)) * scale_factor
    short_grad = lax.optimization_barrier(jnp.sum(short_parts, axis=0)) * scale_factor
    return (clip_out, clip_grad, conv_grad, short_grad)
```

```python
import functools
import jax
import jax.numpy as jnp
from jax import lax
from jax.experimental import pallas as pl
from jax.experimental.pallas import tpu as pltpu
from jax.sharding import PartitionSpec as P

MESH = pl.DeviceIdType.MESH
GROUPS = 32
epsilon = 1e-06
TAPS = [(t, i) for t in range(3) for i in range(3)]
WIDTHS = (768, 768, 768, 768, 512)
STARTS = (0, 768, 1536, 2304, 3072)


def group_total(value):
    lane = lax.broadcasted_iota(jnp.int32, value.shape, 1)
    width = value.shape[1]
    value = value + jnp.where(lane % 2 == 0, pltpu.roll(value, width - 1, 1), pltpu.roll(value, 1, 1))
    return value + jnp.where(lane % 4 < 2, pltpu.roll(value, width - 2, 1), pltpu.roll(value, 2, 1))


def kernel(
    n_dp, n_ctx,
    clip, cot, gain, bias, conv_w, short_w,
    clip_out, clip_grad, conv_grad, short_grad,
    xall, cots, weight, weight_t, taps, back, cot_t,
    sums, sums_in, sums2, sums2_in,
    part, pair_in, ctx_out, ctx_in, total, slots, slots_in, out_buf, grad_buf,
    in_sem, halo_send, halo_recv, s_send, s_recv, s2_send, s2_recv,
    pair_send, pair_recv, a_send, a_recv, b_send, b_recv, out_sem,
):
    f32, bf16 = jnp.float32, jnp.bfloat16
    dp, ctx = lax.axis_index("dp"), lax.axis_index("ctx")
    half = dp % 2
    partner = dp + 1 - 2 * half
    members = 4 * n_ctx * 4 * 96 * 4

    loads = [
        pltpu.make_async_copy(clip, xall.at[2:6], in_sem.at[0]),
        pltpu.make_async_copy(cot, cots.at[0:4, 96:480], in_sem.at[1]),
        pltpu.make_async_copy(conv_w, weight.at[0:3456], in_sem.at[2]),
        pltpu.make_async_copy(short_w, weight.at[3456:3584], in_sem.at[3]),
    ]
    for copy in loads:
        copy.start()

    barrier = pltpu.get_barrier_semaphore()

    def greet_ctx(step, carry):
        pl.semaphore_signal(barrier, inc=1, device_id={"dp": dp, "ctx": (ctx + step) % n_ctx}, device_id_type=MESH)
        return carry

    def greet_dp(step, carry):
        pl.semaphore_signal(barrier, inc=1, device_id={"dp": (dp + step) % n_dp, "ctx": ctx}, device_id_type=MESH)
        return carry

    lax.fori_loop(1, n_ctx, greet_ctx, 0)
    lax.fori_loop(1, n_dp, greet_dp, 0)

    loads[0].wait()
    first = jnp.zeros((8, 128), f32)
    second = jnp.zeros((8, 128), f32)
    for f in range(4):
        value = xall[2 + f].astype(f32).reshape(48, 8, 128)
        first = first + jnp.sum(value, axis=0)
        second = second + jnp.sum(value * value, axis=0)
    sums[0] = first
    sums[1] = second
    sums_in[ctx] = sums[...]

    pl.semaphore_wait(barrier, n_ctx - 1 + n_dp - 1)

    def sums_copy(source, target, send, recv, peer):
        return pltpu.make_async_remote_copy(
            src_ref=source, dst_ref=target.at[ctx], send_sem=send.at[peer], recv_sem=recv.at[ctx],
            device_id={"dp": dp, "ctx": peer}, device_id_type=MESH,
        )

    def sums_arrival(source, target, send, recv, peer):
        return pltpu.make_async_remote_copy(
            src_ref=source, dst_ref=target.at[peer], send_sem=send.at[peer], recv_sem=recv.at[peer],
            device_id={"dp": dp, "ctx": peer}, device_id_type=MESH,
        )

    def each_ctx(body):
        def step(k, carry):
            body((ctx + k) % n_ctx)
            return carry
        lax.fori_loop(1, n_ctx, step, 0)

    each_ctx(lambda peer: sums_copy(sums, sums_in, s_send, s_recv, peer).start())

    after = jnp.minimum(ctx + 1, n_ctx - 1)
    before = jnp.maximum(ctx - 1, 0)
    clip_halo = pltpu.make_async_remote_copy(
        src_ref=clip.at[2:4], dst_ref=xall.at[0:2], send_sem=halo_send.at[0], recv_sem=halo_recv.at[0],
        device_id={"dp": dp, "ctx": after}, device_id_type=MESH,
    )
    cot_halo = pltpu.make_async_remote_copy(
        src_ref=cot.at[0:2], dst_ref=cots.at[4:6, 96:480], send_sem=halo_send.at[1], recv_sem=halo_recv.at[1],
        device_id={"dp": dp, "ctx": before}, device_id_type=MESH,
    )

    @pl.when(ctx < n_ctx - 1)
    def _():
        clip_halo.start()

    @pl.when(ctx > 0)
    def _():
        cot_halo.start()

    cots[:, 0:96] = jnp.zeros((6, 96, 256), bf16)
    cots[:, 480:576] = jnp.zeros((6, 96, 256), bf16)
    taps[:, 0:96] = jnp.zeros((6, 96, 384), bf16)
    taps[:, 480:576] = jnp.zeros((6, 96, 384), bf16)

    @pl.when(ctx == 0)
    def _():
        xall[0] = xall[2]
        xall[1] = xall[2]

    @pl.when(ctx == n_ctx - 1)
    def _():
        cots[4:6, 96:480] = jnp.zeros((2, 384, 256), bf16)

    column = lax.broadcasted_iota(jnp.int32, (384, 128), 0) % 96
    at_left, at_right = column == 0, column == 95

    def from_left(value):
        return jnp.where(at_left, 0.0, pltpu.roll(value, 1, 0))

    def from_right(value):
        return jnp.where(at_right, 0.0, pltpu.roll(value, 383, 0))

    loads[1].wait()
    for f in range(4):
        cot_t[:, f * 384:f * 384 + 384] = cots[f, 96:480].T
    loads[2].wait()
    loads[3].wait()
    for k in range(9):
        weight_t[k * 256:k * 256 + 256] = weight[k * 384:k * 384 + 384].T

    def joined(product):
        return from_right(product[:, 0:128]) + product[:, 128:256] + from_left(product[:, 256:384])

    def back_frame(f, carry):
        rows = jnp.concatenate([cots[f + 2 - t, (2 - i) * 96:(2 - i) * 96 + 384] for t, i in TAPS], axis=1)
        back[f] = joined(jnp.dot(rows, weight_t[...], preferred_element_type=f32))
        return carry

    lax.fori_loop(0, 2, back_frame, 0)

    @pl.when(ctx == 0)
    def _():
        lead = jnp.concatenate([cots[0, (2 - i) * 96:(2 - i) * 96 + 384] for i in range(3)] * 2, axis=1)
        second_rows = jnp.concatenate([cots[1, (2 - i) * 96:(2 - i) * 96 + 384] for i in range(3)], axis=1)
        extra = jnp.dot(lead, weight_t[0:1536], preferred_element_type=f32)
        extra = extra + jnp.dot(second_rows, weight_t[0:768], preferred_element_type=f32)
        back[0] = back[0] + joined(extra)

    each_ctx(lambda peer: sums_arrival(sums, sums_in, s_send, s_recv, peer).wait_recv())
    all_sums = jnp.sum(sums_in[...], axis=(0, 2))
    all_sums = group_total(jnp.concatenate([all_sums, jnp.zeros((6, 128), f32)], axis=0))
    mean = all_sums[0:1] / members
    variance = all_sums[1:2] / members - mean * mean
    inv = lax.rsqrt(variance + epsilon)
    gain_row, bias_row = gain[...], bias[...]

    def standard_of(f):
        return (xall[f].astype(f32) - mean) * inv

    @pl.when(ctx > 0)
    def _():
        clip_halo.wait_recv()

    def hidden_frame(f, carry):
        affine = standard_of(f) * gain_row + bias_row
        hidden = affine * jax.nn.sigmoid(affine)
        taps[f, 96:480, 0:128] = from_left(hidden).astype(bf16)
        taps[f, 96:480, 128:256] = hidden.astype(bf16)
        taps[f, 96:480, 256:384] = from_right(hidden).astype(bf16)
        return carry

    lax.fori_loop(0, 6, hidden_frame, 0)

    def pair_copy(chunk):
        lanes = pl.ds(0, WIDTHS[chunk])
        return pltpu.make_async_remote_copy(
            src_ref=part.at[chunk, :, 1 - half, :, lanes], dst_ref=pair_in.at[chunk, :, :, lanes],
            send_sem=pair_send.at[chunk], recv_sem=pair_recv.at[chunk],
            device_id={"dp": partner, "ctx": ctx}, device_id_type=MESH,
        )

    def ctx_copy(chunk, peer):
        lanes = pl.ds(0, WIDTHS[chunk])
        return pltpu.make_async_remote_copy(
            src_ref=ctx_out.at[chunk, peer, :, lanes], dst_ref=ctx_in.at[chunk, ctx, :, lanes],
            send_sem=a_send.at[chunk, peer], recv_sem=a_recv.at[chunk, ctx],
            device_id={"dp": dp, "ctx": peer}, device_id_type=MESH,
        )

    def ctx_arrival(chunk, peer):
        lanes = pl.ds(0, WIDTHS[chunk])
        return pltpu.make_async_remote_copy(
            src_ref=ctx_out.at[chunk, peer, :, lanes], dst_ref=ctx_in.at[chunk, peer, :, lanes],
            send_sem=a_send.at[chunk, peer], recv_sem=a_recv.at[chunk, peer],
            device_id={"dp": dp, "ctx": peer}, device_id_type=MESH,
        )

    def send_on(chunk):
        width = WIDTHS[chunk]
        pair_copy(chunk).wait_recv()
        ctx_out[chunk, :, :, 0:width] = (
            part[chunk, :, half, :, 0:width] + pair_in[chunk, :, :, 0:width]
        ).astype(bf16)
        each_ctx(lambda peer: ctx_copy(chunk, peer).start())

    for chunk in range(5):
        columns = [
            jnp.concatenate([taps[f + t, i * 96:i * 96 + 384] for f in range(4)], axis=0)
            for t, i in TAPS[2 * chunk:2 * chunk + 2]
        ]
        if chunk == 4:
            columns.append(jnp.concatenate([xall[2 + f] for f in range(4)], axis=0))
        product = jnp.dot(cot_t[...], jnp.concatenate(columns, axis=1), preferred_element_type=f32)
        part[chunk, :, :, :, 0:WIDTHS[chunk]] = product.reshape(n_ctx, 2, 16, WIDTHS[chunk])
        pair_copy(chunk).start()
        if chunk > 0:
            send_on(chunk - 1)

    @pl.when(ctx < n_ctx - 1)
    def _():
        cot_halo.wait_recv()

    back_frame(2, 0)
    send_on(4)
    back_frame(3, 0)

    def norm_frame(f, carry):
        standard = standard_of(f + 2)
        affine = standard * gain_row + bias_row
        logistic = jax.nn.sigmoid(affine)
        grad = back[f] * logistic * (1.0 + affine * (1.0 - logistic)) * gain_row
        back[f] = grad
        return (
            carry[0] + jnp.sum(grad.reshape(48, 8, 128), axis=0),
            carry[1] + jnp.sum((grad * standard).reshape(48, 8, 128), axis=0),
        )

    zero = jnp.zeros((8, 128), f32)
    grad_sum, cross_sum = lax.fori_loop(0, 4, norm_frame, (zero, zero))
    sums2[0] = grad_sum
    sums2[1] = cross_sum
    sums2_in[ctx] = sums2[...]
    each_ctx(lambda peer: sums_copy(sums2, sums2_in, s2_send, s2_recv, peer).start())

    def out_copy(f):
        return pltpu.make_async_copy(out_buf.at[f], clip_out.at[f], out_sem.at[f])

    def grad_copy(f):
        return pltpu.make_async_copy(grad_buf.at[f], clip_grad.at[f], out_sem.at[4 + f])

    def out_frame(f, carry):
        rows = jnp.concatenate([taps[f + t, i * 96:i * 96 + 384] for t, i in TAPS] + [xall[f + 2]], axis=1)
        out_buf[f] = jnp.dot(rows, weight[...], preferred_element_type=f32).astype(bf16)
        out_copy(f).start()
        return carry

    lax.fori_loop(0, 4, out_frame, 0)

    each_ctx(lambda peer: sums_arrival(sums2, sums2_in, s2_send, s2_recv, peer).wait_recv())
    all_sums = jnp.sum(sums2_in[...], axis=(0, 2))
    all_sums = group_total(jnp.concatenate([all_sums, jnp.zeros((6, 128), f32)], axis=0)) / members
    mean_grad, mean_cross = all_sums[0:1], all_sums[1:2]

    def grad_frame(f, carry):
        shortcut = lax.dot_general(
            cots[f, 96:480], weight[3456:3584], (((1,), (1,)), ((), ())), preferred_element_type=f32
        )
        value = (back[f] - mean_grad - standard_of(f + 2) * mean_cross) * inv + shortcut
        grad_buf[f] = value.astype(bf16)
        grad_copy(f).start()
        return carry

    lax.fori_loop(0, 4, grad_frame, 0)

    for chunk in range(5):
        width = WIDTHS[chunk]
        each_ctx(lambda peer: ctx_arrival(chunk, peer).wait_recv())
        start = part[chunk, ctx, half, :, 0:width] + pair_in[chunk, ctx, :, 0:width]
        ctx_in[chunk, ctx, :, 0:width] = jnp.zeros((16, width), bf16)
        value = start
        for source in range(n_ctx):
            value = value + ctx_in[chunk, source, :, 0:width].astype(f32)
        total[:, STARTS[chunk]:STARTS[chunk] + width] = value

    lane = lax.broadcasted_iota(jnp.int32, (16, 128), 1)
    short_lanes = total[:, 3456:3584]
    for owner in range(n_dp):
        base = 108 * owner // 128 * 128
        shift = 108 * owner - base
        piece = total[:, base:base + 256]
        if shift:
            piece = pltpu.roll(piece, 256 - shift, 1)
        tail = pltpu.roll(short_lanes, (108 - 4 * owner) % 128, 1) if (108 - 4 * owner) % 128 else short_lanes
        slots[owner] = jnp.where(lane < 108, piece[:, 0:128], tail)
    slots_in[dp] = slots[dp]

    def slot_copy(peer):
        return pltpu.make_async_remote_copy(
            src_ref=slots.at[peer], dst_ref=slots_in.at[dp], send_sem=b_send.at[peer], recv_sem=b_recv.at[dp],
            device_id={"dp": peer, "ctx": ctx}, device_id_type=MESH,
        )

    def slot_arrival(peer):
        return pltpu.make_async_remote_copy(
            src_ref=slots.at[peer], dst_ref=slots_in.at[peer], send_sem=b_send.at[peer], recv_sem=b_recv.at[peer],
            device_id={"dp": peer, "ctx": ctx}, device_id_type=MESH,
        )

    def each_dp(body):
        def step(k, carry):
            body((dp + k) % n_dp)
            return carry
        lax.fori_loop(1, n_dp, step, 0)

    each_dp(lambda peer: slot_copy(peer).start())

    each_ctx(lambda peer: sums_copy(sums, sums_in, s_send, s_recv, peer).wait_send())
    each_ctx(lambda peer: sums_copy(sums2, sums2_in, s2_send, s2_recv, peer).wait_send())

    @pl.when(ctx < n_ctx - 1)
    def _():
        clip_halo.wait_send()

    @pl.when(ctx > 0)
    def _():
        cot_halo.wait_send()

    for chunk in range(5):
        pair_copy(chunk).wait_send()
        each_ctx(lambda peer: ctx_copy(chunk, peer).wait_send())
    for f in range(4):
        out_copy(f).wait()
        grad_copy(f).wait()

    each_dp(lambda peer: slot_arrival(peer).wait_recv())
    halves = []
    for h in range(2):
        value = slots_in[h]
        for source in range(1, n_dp // 2):
            value = value + slots_in[2 * source + h]
        halves.append(value)
    turned = jnp.concatenate(halves, axis=0).T * (1.0 / (4 * n_ctx * n_dp))
    conv_grad[...] = turned[0:108]
    short_grad[...] = turned[108:112]
    each_dp(lambda peer: slot_copy(peer).wait_send())


def body(n_dp, n_ctx, clip_in, norm_gain, norm_bias, conv_weight, short_weight, out_cotangent):
    f32, bf16 = jnp.float32, jnp.bfloat16
    hbm = pl.BlockSpec(memory_space=pl.ANY)
    vmem = pl.BlockSpec(memory_space=pltpu.VMEM)
    dma = pltpu.SemaphoreType.DMA
    out, grad, conv, short = pl.pallas_call(
        functools.partial(kernel, n_dp, n_ctx),
        out_shape=(
            jax.ShapeDtypeStruct((4, 384, 256), bf16),
            jax.ShapeDtypeStruct((4, 384, 128), bf16),
            jax.ShapeDtypeStruct((108, 32), f32),
            jax.ShapeDtypeStruct((4, 32), f32),
        ),
        in_specs=[hbm, hbm, vmem, vmem, hbm, hbm],
        out_specs=(hbm, hbm, vmem, vmem),
        scratch_shapes=[
            pltpu.VMEM((6, 384, 128), bf16),
            pltpu.VMEM((6, 576, 256), bf16),
            pltpu.VMEM((3584, 256), bf16),
            pltpu.VMEM((2304, 384), bf16),
            pltpu.VMEM((6, 576, 384), bf16),
            pltpu.VMEM((4, 384, 128), f32),
            pltpu.VMEM((256, 1536), bf16),
            pltpu.VMEM((2, 8, 128), f32),
            pltpu.VMEM((n_ctx, 2, 8, 128), f32),
            pltpu.VMEM((2, 8, 128), f32),
            pltpu.VMEM((n_ctx, 2, 8, 128), f32),
            pltpu.VMEM((5, n_ctx, 2, 16, 768), f32),
            pltpu.VMEM((5, n_ctx, 16, 768), f32),
            pltpu.VMEM((5, n_ctx, 16, 768), bf16),
            pltpu.VMEM((5, n_ctx, 16, 768), bf16),
            pltpu.VMEM((16, 3584), f32),
            pltpu.VMEM((n_dp, 16, 128), f32),
            pltpu.VMEM((n_dp, 16, 128), f32),
            pltpu.VMEM((4, 384, 256), bf16),
            pltpu.VMEM((4, 384, 128), bf16),
            dma((4,)), dma((2,)), dma((2,)),
            dma((n_ctx,)), dma((n_ctx,)), dma((n_ctx,)), dma((n_ctx,)),
            dma((5,)), dma((5,)), dma((5, n_ctx)), dma((5, n_ctx)),
            dma((n_dp,)), dma((n_dp,)), dma((8,)),
        ],
        compiler_params=pltpu.CompilerParams(
            collective_id=0, has_side_effects=True, vmem_limit_bytes=52 << 20
        ),
        name="conv_block",
    )(
        clip_in.reshape(4, 384, 128), out_cotangent.reshape(4, 384, 256),
        norm_gain.reshape(1, 128), norm_bias.reshape(1, 128), conv_weight, short_weight,
    )
    return out.reshape(1, 4, 4, 96, 256), grad.reshape(1, 4, 4, 96, 128), conv, short


def solution(mesh):
    return jax.shard_map(
        functools.partial(body, mesh.shape["dp"], mesh.shape["ctx"]),
        mesh=mesh,
        in_specs=(
            P("dp", "ctx", None, None, None),
            P(),
            P(),
            P(),
            P(),
            P("dp", "ctx", None, None, None),
        ),
        out_specs=(
            P("dp", "ctx", None, None, None),
            P("dp", "ctx", None, None, None),
            P("dp", "ctx"),
            P("dp", "ctx"),
        ),
        check_vma=False,
    )
```

```python
import functools
import jax
import jax.numpy as jnp
from jax import lax
from jax.experimental import pallas as pl
from jax.experimental.pallas import tpu as pltpu
from jax.sharding import PartitionSpec as P

MESH = pl.DeviceIdType.MESH
GROUPS = 32
epsilon = 1e-06
TAPS = [(t, i) for t in range(3) for i in range(3)]
CHUNKS = ((2304, 1280), (1152, 1152), (0, 1152))
Y_FIRST = (3, 1)
X_FIRST = (2, 0)


def group_total(value):
    lane = lax.broadcasted_iota(jnp.int32, value.shape, 1)
    width = value.shape[1]
    value = value + jnp.where(lane % 2 == 0, pltpu.roll(value, width - 1, 1), pltpu.roll(value, 1, 1))
    return value + jnp.where(lane % 4 < 2, pltpu.roll(value, width - 2, 1), pltpu.roll(value, 2, 1))


def kernel(
    n_dp, n_ctx,
    clip, cot, gain, bias, conv_w, short_w,
    clip_out, clip_grad, conv_grad, short_grad,
    xall, cots, gain_buf, bias_buf, weight, weight_t, taps, back, edge, edge_in, cot_t,
    sums, sums_in, sums2, sums2_in,
    part, pair_in, total, y_out, y_in, x_out, x_in, step2, step2_in, step3, step3_in,
    out_buf, grad_buf, conv_buf, short_buf,
    in_sem, halo_send, halo_recv, s_send, s_recv, s2_send, s2_recv,
    pair_send, pair_recv, r1_send, r1_recv, r2_send, r2_recv, r3_send, r3_recv, out_sem,
):
    f32, bf16 = jnp.float32, jnp.bfloat16
    dp, ctx = lax.axis_index("dp"), lax.axis_index("ctx")
    z_hi, x, core = dp // 8, dp // 2 % 4, dp % 2
    y, z_lo = ctx // 2, ctx % 2
    members = 4 * n_ctx * 4 * 96 * 4

    def dp_of(z_hi, x, core):
        return (z_hi * 4 + x) * 2 + core

    def ctx_of(y, z_lo):
        return y * 2 + z_lo

    loads = [
        pltpu.make_async_copy(clip, xall.at[2:6], in_sem.at[0]),
        pltpu.make_async_copy(cot, cots.at[:, 96:480], in_sem.at[1]),
        pltpu.make_async_copy(conv_w, weight.at[0:3456], in_sem.at[2]),
        pltpu.make_async_copy(short_w, weight.at[3456:3584], in_sem.at[3]),
        pltpu.make_async_copy(gain, gain_buf, in_sem.at[4]),
        pltpu.make_async_copy(bias, bias_buf, in_sem.at[5]),
    ]
    for copy in loads:
        copy.start()

    barrier = pltpu.get_barrier_semaphore()

    def greet(peer_dp, peer_ctx):
        pl.semaphore_signal(barrier, inc=1, device_id={"dp": peer_dp, "ctx": peer_ctx}, device_id_type=MESH)

    greetings = 0
    for dz in range(4):
        for dl in range(2):
            for dc in range(2):
                if dz or dc:
                    greet(dp_of((z_hi + 4 - dz) % 4, x, (core + dc) % 2), ctx_of(y, (z_lo + dl) % 2))
                    greetings += 1
    for k in range(1, 4):
        greet(dp_of(z_hi, (x + k) % 4, core), ctx)
        greetings += 1
    for k in range(1, n_ctx):
        greet(dp, (ctx + k) % n_ctx)
        greetings += 1

    loads[0].wait()
    first = jnp.zeros((8, 128), f32)
    second = jnp.zeros((8, 128), f32)
    for f in range(4):
        value = xall[2 + f].astype(f32).reshape(48, 8, 128)
        first = first + jnp.sum(value, axis=0)
        second = second + jnp.sum(value * value, axis=0)
    sums[0] = first
    sums[1] = second
    sums_in[ctx] = sums[...]

    pl.semaphore_wait(barrier, greetings)

    def sums_copy(source, target, send, recv, peer):
        return pltpu.make_async_remote_copy(
            src_ref=source, dst_ref=target.at[ctx], send_sem=send.at[peer], recv_sem=recv.at[ctx],
            device_id={"dp": dp, "ctx": peer}, device_id_type=MESH,
        )

    def sums_arrival(source, target, send, recv, peer):
        return pltpu.make_async_remote_copy(
            src_ref=source, dst_ref=target.at[peer], send_sem=send.at[peer], recv_sem=recv.at[peer],
            device_id={"dp": dp, "ctx": peer}, device_id_type=MESH,
        )

    def each_ctx(body):
        for k in range(1, n_ctx):
            body((ctx + k) % n_ctx)

    each_ctx(lambda peer: sums_copy(sums, sums_in, s_send, s_recv, peer).start())

    clip_halo = pltpu.make_async_remote_copy(
        src_ref=xall.at[4:6], dst_ref=xall.at[0:2], send_sem=halo_send.at[0], recv_sem=halo_recv.at[0],
        device_id={"dp": dp, "ctx": jnp.minimum(ctx + 1, n_ctx - 1)}, device_id_type=MESH,
    )
    edge_halo = pltpu.make_async_remote_copy(
        src_ref=edge, dst_ref=edge_in, send_sem=halo_send.at[1], recv_sem=halo_recv.at[1],
        device_id={"dp": dp, "ctx": jnp.maximum(ctx - 1, 0)}, device_id_type=MESH,
    )

    @pl.when(ctx < n_ctx - 1)
    def _():
        clip_halo.start()

    cots[:, 0:96] = jnp.zeros((4, 96, 256), bf16)
    cots[:, 480:576] = jnp.zeros((4, 96, 256), bf16)
    taps[:, 0:96] = jnp.zeros((6, 96, 384), bf16)
    taps[:, 480:576] = jnp.zeros((6, 96, 384), bf16)

    @pl.when(ctx == 0)
    def _():
        xall[0] = xall[2]
        xall[1] = xall[2]

    column = lax.broadcasted_iota(jnp.int32, (384, 128), 0) % 96
    at_left, at_right = column == 0, column == 95

    def from_left(value):
        return jnp.where(at_left, 0.0, pltpu.roll(value, 1, 0))

    def from_right(value):
        return jnp.where(at_right, 0.0, pltpu.roll(value, 383, 0))

    loads[1].wait()
    for f in range(4):
        cot_t[:, f * 384:f * 384 + 384] = cots[f, 96:480].T
    for copy in loads[2:]:
        copy.wait()
    for k in range(9):
        weight_t[k * 256:k * 256 + 256] = weight[k * 384:k * 384 + 384].T

    def back_terms(f, frame_taps):
        rows = jnp.concatenate(
            [cots[f + 2 - t, (2 - i) * 96:(2 - i) * 96 + 384] for t in frame_taps for i in range(3)], axis=1
        )
        turned = weight_t[frame_taps[0] * 768:frame_taps[-1] * 768 + 768]
        product = jnp.dot(rows, turned, preferred_element_type=f32)
        return from_right(product[:, 0:128]) + product[:, 128:256] + from_left(product[:, 256:384])

    ahead = back_terms(-2, (0,)), back_terms(-1, (0, 1))
    back[0] = back_terms(0, (0, 1, 2))

    @pl.when(ctx == 0)
    def _():
        back[0] = back[0] + (ahead[0] + ahead[1])

    edge[0] = ahead[0].astype(bf16)
    edge[1] = ahead[1].astype(bf16)

    @pl.when(ctx > 0)
    def _():
        edge_halo.start()

    back[1] = back_terms(1, (0, 1, 2))

    each_ctx(lambda peer: sums_arrival(sums, sums_in, s_send, s_recv, peer).wait_recv())
    all_sums = jnp.sum(sums_in[...], axis=(0, 2))
    all_sums = group_total(jnp.concatenate([all_sums, jnp.zeros((6, 128), f32)], axis=0))
    mean = all_sums[0:1] / members
    variance = all_sums[1:2] / members - mean * mean
    inv = lax.rsqrt(variance + epsilon)
    gain_row, bias_row = gain_buf[...], bias_buf[...]

    def standard_of(f):
        return (xall[f].astype(f32) - mean) * inv

    def hidden_frame(f, carry):
        affine = standard_of(f) * gain_row + bias_row
        hidden = affine * jax.nn.sigmoid(affine)
        taps[f, 96:480, 0:128] = from_left(hidden).astype(bf16)
        taps[f, 96:480, 128:256] = hidden.astype(bf16)
        taps[f, 96:480, 256:384] = from_right(hidden).astype(bf16)
        return carry

    lax.fori_loop(2, 6, hidden_frame, 0)

    def pair_copy(chunk):
        lanes = pl.ds(0, CHUNKS[chunk][1])
        return pltpu.make_async_remote_copy(
            src_ref=part.at[chunk, :, 1 - core, :, lanes], dst_ref=pair_in.at[chunk, :, :, lanes],
            send_sem=pair_send.at[chunk], recv_sem=pair_recv.at[chunk],
            device_id={"dp": dp + 1 - 2 * core, "ctx": ctx}, device_id_type=MESH,
        )

    def multiply(chunk):
        t = 2 - chunk
        columns = [
            jnp.concatenate([taps[f + t, i * 96:i * 96 + 384] for f in range(4)], axis=0) for i in range(3)
        ]
        if chunk == 0:
            columns.append(jnp.concatenate([xall[2 + f] for f in range(4)], axis=0))
        width = CHUNKS[chunk][1]
        product = jnp.dot(cot_t[...], jnp.concatenate(columns, axis=1), preferred_element_type=f32)
        part[chunk, :, :, :, 0:width] = product.reshape(n_ctx, 2, 16, width)
        pair_copy(chunk).start()

    def add_pair(chunk):
        start, width = CHUNKS[chunk]
        pair_copy(chunk).wait_recv()
        value = part[chunk, :, core, :, 0:width] + pair_in[chunk, :, :, 0:width]
        total[:, start:start + width] = value.reshape(n_ctx * 16, width)

    def peer_at(along_y, k):
        if along_y:
            place = (y + k) % 4
            return place, {"dp": dp, "ctx": ctx_of(place, z_lo)}
        place = (x + k) % 4
        return place, {"dp": dp_of(z_hi, place, core), "ctx": ctx}

    def first_step(quarter, k, arriving=False):
        along_y = quarter in Y_FIRST
        source, target = (y_out, y_in) if along_y else (x_out, x_in)
        row = (Y_FIRST if along_y else X_FIRST).index(quarter)
        place, device = peer_at(along_y, k)
        slot = place if arriving else (y if along_y else x)
        return pltpu.make_async_remote_copy(
            src_ref=source.at[row, place], dst_ref=target.at[row, slot],
            send_sem=r1_send.at[quarter, place], recv_sem=r1_recv.at[quarter, slot],
            device_id=device, device_id_type=MESH,
        )

    def second_step(quarter, k, arriving=False):
        along_y = quarter in X_FIRST
        place, device = peer_at(along_y, k)
        slot = place if arriving else (y if along_y else x)
        return pltpu.make_async_remote_copy(
            src_ref=step2.at[quarter, place], dst_ref=step2_in.at[quarter, slot],
            send_sem=r2_send.at[quarter, place], recv_sem=r2_recv.at[quarter, slot],
            device_id=device, device_id_type=MESH,
        )

    def third_step(quarter, to_lo, to_core):
        return pltpu.make_async_remote_copy(
            src_ref=step3.at[quarter, to_lo, to_core], dst_ref=step3_in.at[z_hi * 2 + z_lo, core],
            send_sem=r3_send.at[quarter, to_lo, to_core], recv_sem=r3_recv.at[z_hi * 2 + z_lo, core],
            device_id={"dp": dp_of(quarter, x, to_core), "ctx": ctx_of(y, to_lo)}, device_id_type=MESH,
        )

    def third_arrival(from_z, from_core):
        return pltpu.make_async_remote_copy(
            src_ref=step3.at[0, 0, 0], dst_ref=step3_in.at[from_z, from_core],
            send_sem=r3_send.at[0, 0, 0], recv_sem=r3_recv.at[from_z, from_core],
            device_id={"dp": dp_of(from_z // 2, x, from_core), "ctx": ctx_of(y, from_z % 2)}, device_id_type=MESH,
        )

    lane = lax.broadcasted_iota(jnp.int32, (128, 128), 1)

    def begin(quarter):
        short_lanes = total[:, 3456:3584]
        for place in range(8):
            owner = 8 * quarter + place
            base = 108 * owner // 128 * 128
            shift = 108 * owner - base
            value = total[:, base:base + 256]
            if shift:
                value = pltpu.roll(value, 256 - shift, 1)
            tail = (108 - 4 * owner) % 128
            tail = pltpu.roll(short_lanes, tail, 1) if tail else short_lanes
            value = jnp.where(lane < 108, value[:, 0:128], tail).astype(bf16)
            if quarter in Y_FIRST:
                y_out[Y_FIRST.index(quarter), :, :, place * 128:place * 128 + 128] = value.reshape(4, 32, 128)
            else:
                at = place % 2 * 128
                x_out[X_FIRST.index(quarter), place // 2, :, at:at + 128] = value
        for k in (1, 3, 2):
            first_step(quarter, k).start()
        if quarter in Y_FIRST:
            y_in[Y_FIRST.index(quarter), y] = y_out[Y_FIRST.index(quarter), y]
        else:
            x_in[X_FIRST.index(quarter), x] = x_out[X_FIRST.index(quarter), x]

    def go_on(quarter):
        for k in (1, 3, 2):
            first_step(quarter, k, arriving=True).wait_recv()
        along_y = quarter in Y_FIRST
        arrived = y_in if along_y else x_in
        row = (Y_FIRST if along_y else X_FIRST).index(quarter)
        value = arrived[row, 0].astype(f32)
        for place in range(1, 4):
            value = value + arrived[row, place].astype(f32)
        if along_y:
            for place in range(4):
                step2[quarter, place] = value[:, place * 256:place * 256 + 256]
        else:
            step2[quarter] = value.reshape(4, 32, 256)
        for k in (1, 3, 2):
            second_step(quarter, k).start()
        own = x if along_y else y
        step2_in[quarter, own] = step2[quarter, own]

    def finish(quarter):
        for k in (1, 3, 2):
            second_step(quarter, k, arriving=True).wait_recv()
        value = step2_in[quarter, 0]
        for place in range(1, 4):
            value = value + step2_in[quarter, place]
        for to_lo in range(2):
            for to_core in range(2):
                step3[quarter, to_lo, to_core] = value[to_lo * 16:to_lo * 16 + 16, to_core * 128:to_core * 128 + 128]
                mine = (z_hi == quarter) & (z_lo == to_lo) & (core == to_core)

                @pl.when(jnp.logical_not(mine))
                def _():
                    third_step(quarter, to_lo, to_core).start()

                @pl.when(mine)
                def _():
                    step3_in[z_hi * 2 + z_lo, core] = step3[quarter, to_lo, to_core]

    multiply(0)

    @pl.when(ctx > 0)
    def _():
        clip_halo.wait_recv()

    lax.fori_loop(0, 2, hidden_frame, 0)
    multiply(1)
    add_pair(0)
    begin(3)
    multiply(2)
    add_pair(1)
    begin(2)
    back[2] = back_terms(2, (1, 2))
    add_pair(2)
    begin(1)
    begin(0)

    back[3] = back_terms(3, (2,))

    @pl.when(ctx < n_ctx - 1)
    def _():
        edge_halo.wait_recv()
        back[2] = back[2] + edge_in[0].astype(f32)
        back[3] = back[3] + edge_in[1].astype(f32)

    def norm_frame(f, carry):
        standard = standard_of(f + 2)
        affine = standard * gain_row + bias_row
        logistic = jax.nn.sigmoid(affine)
        grad = back[f] * logistic * (1.0 + affine * (1.0 - logistic)) * gain_row
        back[f] = grad
        return (
            carry[0] + jnp.sum(grad.reshape(48, 8, 128), axis=0),
            carry[1] + jnp.sum((grad * standard).reshape(48, 8, 128), axis=0),
        )

    zero = jnp.zeros((8, 128), f32)
    grad_sum, cross_sum = lax.fori_loop(0, 4, norm_frame, (zero, zero))
    sums2[0] = grad_sum
    sums2[1] = cross_sum
    sums2_in[ctx] = sums2[...]
    each_ctx(lambda peer: sums_copy(sums2, sums2_in, s2_send, s2_recv, peer).start())

    def out_copy(f):
        return pltpu.make_async_copy(out_buf.at[f], clip_out.at[f], out_sem.at[f])

    def grad_copy(f):
        return pltpu.make_async_copy(grad_buf.at[f], clip_grad.at[f], out_sem.at[4 + f])

    def out_frame(f, carry):
        rows = jnp.concatenate([taps[f + t, i * 96:i * 96 + 384] for t, i in TAPS] + [xall[f + 2]], axis=1)
        out_buf[f] = jnp.dot(rows, weight[...], preferred_element_type=f32).astype(bf16)
        out_copy(f).start()
        return carry

    go_on(3)
    go_on(2)
    lax.fori_loop(0, 1, out_frame, 0)
    go_on(1)
    go_on(0)
    lax.fori_loop(1, 3, out_frame, 0)
    for quarter in (3, 2, 1, 0):
        finish(quarter)
    lax.fori_loop(3, 4, out_frame, 0)

    each_ctx(lambda peer: sums_arrival(sums2, sums2_in, s2_send, s2_recv, peer).wait_recv())
    all_sums = jnp.sum(sums2_in[...], axis=(0, 2))
    all_sums = group_total(jnp.concatenate([all_sums, jnp.zeros((6, 128), f32)], axis=0)) / members
    mean_grad, mean_cross = all_sums[0:1], all_sums[1:2]

    def grad_frame(f, carry):
        shortcut = lax.dot_general(
            cots[f, 96:480], weight[3456:3584], (((1,), (1,)), ((), ())), preferred_element_type=f32
        )
        value = (back[f] - mean_grad - standard_of(f + 2) * mean_cross) * inv + shortcut
        grad_buf[f] = value.astype(bf16)
        grad_copy(f).start()
        return carry

    lax.fori_loop(0, 4, grad_frame, 0)

    each_ctx(lambda peer: sums_copy(sums, sums_in, s_send, s_recv, peer).wait_send())
    each_ctx(lambda peer: sums_copy(sums2, sums2_in, s2_send, s2_recv, peer).wait_send())

    @pl.when(ctx < n_ctx - 1)
    def _():
        clip_halo.wait_send()

    @pl.when(ctx > 0)
    def _():
        edge_halo.wait_send()

    for chunk in range(3):
        pair_copy(chunk).wait_send()
    for quarter in range(4):
        for k in range(1, 4):
            first_step(quarter, k).wait_send()
            second_step(quarter, k).wait_send()
    for f in range(4):
        out_copy(f).wait()
        grad_copy(f).wait()
    for quarter in range(4):
        for to_lo in range(2):
            for to_core in range(2):
                mine = (z_hi == quarter) & (z_lo == to_lo) & (core == to_core)

                @pl.when(jnp.logical_not(mine))
                def _():
                    third_step(quarter, to_lo, to_core).wait_send()

    for from_z in range(8):
        for from_core in range(2):
            mine = (z_hi * 2 + z_lo == from_z) & (core == from_core)

            @pl.when(jnp.logical_not(mine))
            def _():
                third_arrival(from_z, from_core).wait_recv()

    halves = []
    for h in range(2):
        value = step3_in[0, h]
        for from_z in range(1, 8):
            value = value + step3_in[from_z, h]
        halves.append(value)
    value = jnp.concatenate(halves, axis=0) * (1.0 / (4 * n_ctx * n_dp))
    conv_buf[...] = value[:, 0:108]
    short_buf[...] = value.T[108:112]
    ends = [
        pltpu.make_async_copy(conv_buf, conv_grad, out_sem.at[8]),
        pltpu.make_async_copy(short_buf, short_grad, out_sem.at[9]),
    ]
    for copy in ends:
        copy.start()
    for copy in ends:
        copy.wait()


def store(*refs):
    sources, targets, sems = refs[0:4], refs[4:8], refs[8]
    copies = [pltpu.make_async_copy(sources[k], targets[k], sems.at[k]) for k in range(4)]
    for copy in copies:
        copy.start()
    for copy in copies:
        copy.wait()


def body(n_dp, n_ctx, clip_in, norm_gain, norm_bias, conv_weight, short_weight, out_cotangent):
    f32, bf16 = jnp.float32, jnp.bfloat16
    anywhere = pl.BlockSpec(memory_space=pl.ANY)
    hbm = pl.BlockSpec(memory_space=pltpu.HBM)
    dma = pltpu.SemaphoreType.DMA
    shapes = (
        jax.ShapeDtypeStruct((4, 384, 256), bf16),
        jax.ShapeDtypeStruct((4, 384, 128), bf16),
        jax.ShapeDtypeStruct((32, 108), f32),
        jax.ShapeDtypeStruct((4, 32), f32),
    )
    results = pl.pallas_call(
        functools.partial(kernel, n_dp, n_ctx),
        out_shape=shapes,
        in_specs=[hbm] * 6,
        out_specs=(anywhere,) * 4,
        scratch_shapes=[
            pltpu.VMEM((6, 384, 128), bf16),
            pltpu.VMEM((4, 576, 256), bf16),
            pltpu.VMEM((1, 128), f32),
            pltpu.VMEM((1, 128), f32),
            pltpu.VMEM((3584, 256), bf16),
            pltpu.VMEM((2304, 384), bf16),
            pltpu.VMEM((6, 576, 384), bf16),
            pltpu.VMEM((4, 384, 128), f32),
            pltpu.VMEM((2, 384, 128), bf16),
            pltpu.VMEM((2, 384, 128), bf16),
            pltpu.VMEM((256, 1536), bf16),
            pltpu.VMEM((2, 8, 128), f32),
            pltpu.VMEM((n_ctx, 2, 8, 128), f32),
            pltpu.VMEM((2, 8, 128), f32),
            pltpu.VMEM((n_ctx, 2, 8, 128), f32),
            pltpu.VMEM((3, n_ctx, 2, 16, 1280), f32),
            pltpu.VMEM((3, n_ctx, 16, 1280), f32),
            pltpu.VMEM((128, 3584), f32),
            pltpu.VMEM((2, 4, 32, 1024), bf16),
            pltpu.VMEM((2, 4, 32, 1024), bf16),
            pltpu.VMEM((2, 4, 128, 256), bf16),
            pltpu.VMEM((2, 4, 128, 256), bf16),
            pltpu.VMEM((4, 4, 32, 256), f32),
            pltpu.VMEM((4, 4, 32, 256), f32),
            pltpu.VMEM((4, 2, 2, 16, 128), f32),
            pltpu.VMEM((8, 2, 16, 128), f32),
            pltpu.VMEM((4, 384, 256), bf16),
            pltpu.VMEM((4, 384, 128), bf16),
            pltpu.VMEM((32, 108), f32),
            pltpu.VMEM((4, 32), f32),
            dma((6,)), dma((2,)), dma((2,)),
            dma((n_ctx,)), dma((n_ctx,)), dma((n_ctx,)), dma((n_ctx,)),
            dma((3,)), dma((3,)), dma((4, 4)), dma((4, 4)), dma((4, 4)), dma((4, 4)),
            dma((4, 2, 2)), dma((8, 2)), dma((10,)),
        ],
        compiler_params=pltpu.CompilerParams(
            collective_id=0, has_side_effects=True, vmem_limit_bytes=48 << 20
        ),
        name="conv_block",
    )(
        *[pltpu.with_memory_space_constraint(v, pltpu.HBM) for v in (clip_in.reshape(4, 384, 128), out_cotangent.reshape(4, 384, 256),
        norm_gain.reshape(1, 128), norm_bias.reshape(1, 128), conv_weight, short_weight)]
    )
    out, grad, conv, short = pl.pallas_call(
        store,
        out_shape=shapes,
        in_specs=[anywhere] * 4,
        out_specs=(anywhere,) * 4,
        scratch_shapes=[dma((4,))],
        name="store",
    )(*[pltpu.with_memory_space_constraint(v, pltpu.VMEM) for v in results])
    return out.reshape(1, 4, 4, 96, 256), grad.reshape(1, 4, 4, 96, 128), conv.T, short


def solution(mesh):
    return jax.shard_map(
        functools.partial(body, mesh.shape["dp"], mesh.shape["ctx"]),
        mesh=mesh,
        in_specs=(
            P("dp", "ctx", None, None, None),
            P(),
            P(),
            P(),
            P(),
            P("dp", "ctx", None, None, None),
        ),
        out_specs=(
            P("dp", "ctx", None, None, None),
            P("dp", "ctx", None, None, None),
            P("dp", "ctx"),
            P("dp", "ctx"),
        ),
        check_vma=False,
    )
```

```python
import functools
import jax
import jax.numpy as jnp
from jax import lax
from jax.experimental import pallas as pl
from jax.experimental.pallas import tpu as pltpu
from jax.sharding import PartitionSpec as P

MESH = pl.DeviceIdType.MESH
GROUPS = 32
epsilon = 1e-06
TAPS = [(t, i) for t in range(3) for i in range(3)]
CHUNKS = ((2304, 1280), (1152, 1152), (0, 1152))
Y_FIRST, X_FIRST = 0, 1


def group_total(value):
    lane = lax.broadcasted_iota(jnp.int32, value.shape, 1)
    width = value.shape[1]
    value = value + jnp.where(lane % 2 == 0, pltpu.roll(value, width - 1, 1), pltpu.roll(value, 1, 1))
    return value + jnp.where(lane % 4 < 2, pltpu.roll(value, width - 2, 1), pltpu.roll(value, 2, 1))


def kernel(
    n_dp, n_ctx,
    clip, cot, gain, bias, conv_w, short_w,
    clip_out, clip_grad, conv_grad, short_grad,
    xall, cots, gain_buf, bias_buf, weight, weight_t, taps, back, edge, edge_in, cot_t,
    sums, sums_in, sums2, sums2_in,
    part, pair_in, total, y_out, y_in, x_out, x_in, step2, step2_in, step3, step3_in,
    out_buf, grad_buf, conv_buf, short_buf,
    in_sem, halo_send, halo_recv, s_send, s_recv, s2_send, s2_recv,
    pair_send, pair_recv, r1_send, r1_recv, r2_send, r2_recv, r3_send, r3_recv, out_sem,
):
    f32, bf16 = jnp.float32, jnp.bfloat16
    dp, ctx = lax.axis_index("dp"), lax.axis_index("ctx")
    z_hi, x, core = dp // 8, dp // 2 % 4, dp % 2
    y, z_lo = ctx // 2, ctx % 2
    members = 4 * n_ctx * 4 * 96 * 4

    def dp_of(z_hi, x, core):
        return (z_hi * 4 + x) * 2 + core

    def ctx_of(y, z_lo):
        return y * 2 + z_lo

    loads = [
        pltpu.make_async_copy(clip, xall.at[2:6], in_sem.at[0]),
        pltpu.make_async_copy(cot, cots.at[:, 96:480], in_sem.at[1]),
        pltpu.make_async_copy(conv_w, weight.at[0:3456], in_sem.at[2]),
        pltpu.make_async_copy(short_w, weight.at[3456:3584], in_sem.at[3]),
        pltpu.make_async_copy(gain, gain_buf, in_sem.at[4]),
        pltpu.make_async_copy(bias, bias_buf, in_sem.at[5]),
    ]
    for copy in loads:
        copy.start()

    barrier = pltpu.get_barrier_semaphore()

    def greet(peer_dp, peer_ctx):
        pl.semaphore_signal(barrier, inc=1, device_id={"dp": peer_dp, "ctx": peer_ctx}, device_id_type=MESH)

    greetings = 0
    for dz in range(4):
        for dl in range(2):
            for dc in range(2):
                if dz or dc:
                    greet(dp_of((z_hi + 4 - dz) % 4, x, (core + dc) % 2), ctx_of(y, (z_lo + dl) % 2))
                    greetings += 1
    for k in range(1, 4):
        greet(dp_of(z_hi, (x + k) % 4, core), ctx)
        greetings += 1
    for k in range(1, n_ctx):
        greet(dp, (ctx + k) % n_ctx)
        greetings += 1

    loads[0].wait()
    first = jnp.zeros((8, 128), f32)
    second = jnp.zeros((8, 128), f32)
    for f in range(4):
        value = xall[2 + f].astype(f32).reshape(48, 8, 128)
        first = first + jnp.sum(value, axis=0)
        second = second + jnp.sum(value * value, axis=0)
    sums[0] = first
    sums[1] = second
    sums_in[ctx] = sums[...]

    pl.semaphore_wait(barrier, greetings)

    def sums_copy(source, target, send, recv, peer):
        return pltpu.make_async_remote_copy(
            src_ref=source, dst_ref=target.at[ctx], send_sem=send.at[peer], recv_sem=recv.at[ctx],
            device_id={"dp": dp, "ctx": peer}, device_id_type=MESH,
        )

    def sums_arrival(source, target, send, recv, peer):
        return pltpu.make_async_remote_copy(
            src_ref=source, dst_ref=target.at[peer], send_sem=send.at[peer], recv_sem=recv.at[peer],
            device_id={"dp": dp, "ctx": peer}, device_id_type=MESH,
        )

    def each_ctx(body):
        for k in range(1, n_ctx):
            body((ctx + k) % n_ctx)

    each_ctx(lambda peer: sums_copy(sums, sums_in, s_send, s_recv, peer).start())

    clip_halo = pltpu.make_async_remote_copy(
        src_ref=xall.at[4:6], dst_ref=xall.at[0:2], send_sem=halo_send.at[0], recv_sem=halo_recv.at[0],
        device_id={"dp": dp, "ctx": jnp.minimum(ctx + 1, n_ctx - 1)}, device_id_type=MESH,
    )
    edge_halo = pltpu.make_async_remote_copy(
        src_ref=edge, dst_ref=edge_in, send_sem=halo_send.at[1], recv_sem=halo_recv.at[1],
        device_id={"dp": dp, "ctx": jnp.maximum(ctx - 1, 0)}, device_id_type=MESH,
    )

    @pl.when(ctx < n_ctx - 1)
    def _():
        clip_halo.start()

    cots[:, 0:96] = jnp.zeros((4, 96, 256), bf16)
    cots[:, 480:576] = jnp.zeros((4, 96, 256), bf16)
    taps[:, 0:96] = jnp.zeros((6, 96, 384), bf16)
    taps[:, 480:576] = jnp.zeros((6, 96, 384), bf16)

    @pl.when(ctx == 0)
    def _():
        xall[0] = xall[2]
        xall[1] = xall[2]

    column = lax.broadcasted_iota(jnp.int32, (384, 128), 0) % 96
    at_left, at_right = column == 0, column == 95

    def from_left(value):
        return jnp.where(at_left, 0.0, pltpu.roll(value, 1, 0))

    def from_right(value):
        return jnp.where(at_right, 0.0, pltpu.roll(value, 383, 0))

    loads[1].wait()
    for f in range(4):
        cot_t[:, f * 384:f * 384 + 384] = cots[f, 96:480].T
    for copy in loads[2:]:
        copy.wait()
    for k in range(9):
        weight_t[k * 256:k * 256 + 256] = weight[k * 384:k * 384 + 384].T

    def back_terms(f, frame_taps):
        rows = jnp.concatenate(
            [cots[f + 2 - t, (2 - i) * 96:(2 - i) * 96 + 384] for t in frame_taps for i in range(3)], axis=1
        )
        turned = weight_t[frame_taps[0] * 768:frame_taps[-1] * 768 + 768]
        product = jnp.dot(rows, turned, preferred_element_type=f32)
        return from_right(product[:, 0:128]) + product[:, 128:256] + from_left(product[:, 256:384])

    ahead = back_terms(-2, (0,)), back_terms(-1, (0, 1))
    back[0] = back_terms(0, (0, 1, 2))

    @pl.when(ctx == 0)
    def _():
        back[0] = back[0] + (ahead[0] + ahead[1])

    edge[0] = ahead[0].astype(bf16)
    edge[1] = ahead[1].astype(bf16)

    @pl.when(ctx > 0)
    def _():
        edge_halo.start()

    back[1] = back_terms(1, (0, 1, 2))

    each_ctx(lambda peer: sums_arrival(sums, sums_in, s_send, s_recv, peer).wait_recv())
    all_sums = jnp.sum(sums_in[...], axis=(0, 2))
    all_sums = group_total(jnp.concatenate([all_sums, jnp.zeros((6, 128), f32)], axis=0))
    mean = all_sums[0:1] / members
    variance = all_sums[1:2] / members - mean * mean
    inv = lax.rsqrt(variance + epsilon)
    gain_row, bias_row = gain_buf[...], bias_buf[...]

    def standard_of(f):
        return (xall[f].astype(f32) - mean) * inv

    def hidden_frame(f, carry):
        affine = standard_of(f) * gain_row + bias_row
        hidden = affine * jax.nn.sigmoid(affine)
        taps[f, 96:480, 0:128] = from_left(hidden).astype(bf16)
        taps[f, 96:480, 128:256] = hidden.astype(bf16)
        taps[f, 96:480, 256:384] = from_right(hidden).astype(bf16)
        return carry

    lax.fori_loop(2, 6, hidden_frame, 0)

    def pair_copy(chunk):
        lanes = pl.ds(0, CHUNKS[chunk][1])
        return pltpu.make_async_remote_copy(
            src_ref=part.at[chunk, :, 1 - core, :, lanes], dst_ref=pair_in.at[chunk, :, :, lanes],
            send_sem=pair_send.at[chunk], recv_sem=pair_recv.at[chunk],
            device_id={"dp": dp + 1 - 2 * core, "ctx": ctx}, device_id_type=MESH,
        )

    def multiply(chunk):
        t = 2 - chunk
        columns = [
            jnp.concatenate([taps[f + t, i * 96:i * 96 + 384] for f in range(4)], axis=0) for i in range(3)
        ]
        if chunk == 0:
            columns.append(jnp.concatenate([xall[2 + f] for f in range(4)], axis=0))
        width = CHUNKS[chunk][1]
        product = jnp.dot(cot_t[...], jnp.concatenate(columns, axis=1), preferred_element_type=f32)
        part[chunk, :, :, :, 0:width] = product.reshape(n_ctx, 2, 16, width)
        pair_copy(chunk).start()

    def add_pair(chunk):
        start, width = CHUNKS[chunk]
        pair_copy(chunk).wait_recv()
        value = part[chunk, :, core, :, 0:width] + pair_in[chunk, :, :, 0:width]
        total[:, start:start + width] = value.reshape(n_ctx * 16, width)

    def peer_at(along_y, k):
        if along_y:
            place = (y + k) % 4
            return place, {"dp": dp, "ctx": ctx_of(place, z_lo)}
        place = (x + k) % 4
        return place, {"dp": dp_of(z_hi, place, core), "ctx": ctx}

    def first_step(quarter, kind, k, arriving=False):
        along_y = kind == Y_FIRST
        source, target = (y_out, y_in) if along_y else (x_out, x_in)
        place, device = peer_at(along_y, k)
        slot = place if arriving else (y if along_y else x)
        return pltpu.make_async_remote_copy(
            src_ref=source.at[quarter, place], dst_ref=target.at[quarter, slot],
            send_sem=r1_send.at[quarter, kind, place], recv_sem=r1_recv.at[quarter, kind, slot],
            device_id=device, device_id_type=MESH,
        )

    def second_step(quarter, kind, k, arriving=False):
        along_y = kind == X_FIRST
        place, device = peer_at(along_y, k)
        slot = place if arriving else (y if along_y else x)
        return pltpu.make_async_remote_copy(
            src_ref=step2.at[quarter, kind, place], dst_ref=step2_in.at[quarter, kind, slot],
            send_sem=r2_send.at[quarter, kind, place], recv_sem=r2_recv.at[quarter, kind, slot],
            device_id=device, device_id_type=MESH,
        )

    def third_step(quarter, to_lo, to_core):
        return pltpu.make_async_remote_copy(
            src_ref=step3.at[quarter, to_lo, to_core], dst_ref=step3_in.at[z_hi * 2 + z_lo, core],
            send_sem=r3_send.at[quarter, to_lo, to_core], recv_sem=r3_recv.at[z_hi * 2 + z_lo, core],
            device_id={"dp": dp_of(quarter, x, to_core), "ctx": ctx_of(y, to_lo)}, device_id_type=MESH,
        )

    def third_arrival(from_z, from_core):
        return pltpu.make_async_remote_copy(
            src_ref=step3.at[0, 0, 0], dst_ref=step3_in.at[from_z, from_core],
            send_sem=r3_send.at[0, 0, 0], recv_sem=r3_recv.at[from_z, from_core],
            device_id={"dp": dp_of(from_z // 2, x, from_core), "ctx": ctx_of(y, from_z % 2)}, device_id_type=MESH,
        )

    lane = lax.broadcasted_iota(jnp.int32, (128, 128), 1)

    def begin(quarter):
        short_lanes = total[:, 3456:3584]
        for place in range(8):
            owner = 8 * quarter + place
            base = 108 * owner // 128 * 128
            shift = 108 * owner - base
            value = total[:, base:base + 256]
            if shift:
                value = pltpu.roll(value, 256 - shift, 1)
            tail = (108 - 4 * owner) % 128
            tail = pltpu.roll(short_lanes, tail, 1) if tail else short_lanes
            value = jnp.where(lane < 108, value[:, 0:128], tail).astype(bf16)
            if place % 2 == Y_FIRST:
                at = place // 2 * 128
                y_out[quarter, :, :, at:at + 128] = value.reshape(4, 32, 128)
            else:
                x_out[quarter, place // 2] = value
        for k in (2, 1, 3):
            first_step(quarter, Y_FIRST, k).start()
            first_step(quarter, X_FIRST, k).start()
        y_in[quarter, y] = y_out[quarter, y]
        x_in[quarter, x] = x_out[quarter, x]

    def go_on(quarter):
        for kind, arrived in ((Y_FIRST, y_in), (X_FIRST, x_in)):
            for k in (1, 3, 2):
                first_step(quarter, kind, k, arriving=True).wait_recv()
            value = arrived[quarter, 0].astype(f32)
            for place in range(1, 4):
                value = value + arrived[quarter, place].astype(f32)
            if kind == Y_FIRST:
                for place in range(4):
                    step2[quarter, kind, place] = value[:, place * 128:place * 128 + 128]
            else:
                step2[quarter, kind] = value.reshape(4, 32, 128)
            for k in (2, 1, 3):
                second_step(quarter, kind, k).start()
            own = x if kind == Y_FIRST else y
            step2_in[quarter, kind, own] = step2[quarter, kind, own]

    def finish(quarter):
        for kind in (Y_FIRST, X_FIRST):
            to_core = kind
            for k in (1, 3, 2):
                second_step(quarter, kind, k, arriving=True).wait_recv()
            value = step2_in[quarter, kind, 0]
            for place in range(1, 4):
                value = value + step2_in[quarter, kind, place]
            value = value.astype(step3.dtype)
            for to_lo in range(2):
                step3[quarter, to_lo, to_core] = value[to_lo * 16:to_lo * 16 + 16]
                mine = (z_hi == quarter) & (z_lo == to_lo) & (core == to_core)

                @pl.when(jnp.logical_not(mine))
                def _():
                    third_step(quarter, to_lo, to_core).start()

                @pl.when(mine)
                def _():
                    step3_in[z_hi * 2 + z_lo, core] = step3[quarter, to_lo, to_core]

    multiply(0)

    @pl.when(ctx > 0)
    def _():
        clip_halo.wait_recv()

    lax.fori_loop(0, 2, hidden_frame, 0)
    multiply(1)
    add_pair(0)
    begin(3)
    multiply(2)
    add_pair(1)
    begin(2)
    back[2] = back_terms(2, (1, 2))
    add_pair(2)
    begin(1)
    begin(0)

    back[3] = back_terms(3, (2,))

    @pl.when(ctx < n_ctx - 1)
    def _():
        edge_halo.wait_recv()
        back[2] = back[2] + edge_in[0].astype(f32)
        back[3] = back[3] + edge_in[1].astype(f32)

    def norm_frame(f, carry):
        standard = standard_of(f + 2)
        affine = standard * gain_row + bias_row
        logistic = jax.nn.sigmoid(affine)
        grad = back[f] * logistic * (1.0 + affine * (1.0 - logistic)) * gain_row
        back[f] = grad
        return (
            carry[0] + jnp.sum(grad.reshape(48, 8, 128), axis=0),
            carry[1] + jnp.sum((grad * standard).reshape(48, 8, 128), axis=0),
        )

    zero = jnp.zeros((8, 128), f32)
    grad_sum, cross_sum = lax.fori_loop(0, 4, norm_frame, (zero, zero))
    sums2[0] = grad_sum
    sums2[1] = cross_sum
    sums2_in[ctx] = sums2[...]
    each_ctx(lambda peer: sums_copy(sums2, sums2_in, s2_send, s2_recv, peer).start())

    def out_copy(f):
        return pltpu.make_async_copy(out_buf.at[f], clip_out.at[f], out_sem.at[f])

    def grad_copy(f):
        return pltpu.make_async_copy(grad_buf.at[f], clip_grad.at[f], out_sem.at[4 + f])

    def out_frame(f, carry):
        rows = jnp.concatenate([taps[f + t, i * 96:i * 96 + 384] for t, i in TAPS] + [xall[f + 2]], axis=1)
        out_buf[f] = jnp.dot(rows, weight[...], preferred_element_type=f32).astype(bf16)
        out_copy(f).start()
        return carry

    go_on(3)
    go_on(2)
    lax.fori_loop(0, 2, out_frame, 0)
    go_on(1)
    go_on(0)
    finish(3)
    finish(2)
    lax.fori_loop(2, 3, out_frame, 0)
    finish(1)
    finish(0)
    lax.fori_loop(3, 4, out_frame, 0)

    each_ctx(lambda peer: sums_arrival(sums2, sums2_in, s2_send, s2_recv, peer).wait_recv())
    all_sums = jnp.sum(sums2_in[...], axis=(0, 2))
    all_sums = group_total(jnp.concatenate([all_sums, jnp.zeros((6, 128), f32)], axis=0)) / members
    mean_grad, mean_cross = all_sums[0:1], all_sums[1:2]

    def grad_frame(f, carry):
        shortcut = lax.dot_general(
            cots[f, 96:480], weight[3456:3584], (((1,), (1,)), ((), ())), preferred_element_type=f32
        )
        value = (back[f] - mean_grad - standard_of(f + 2) * mean_cross) * inv + shortcut
        grad_buf[f] = value.astype(bf16)
        grad_copy(f).start()
        return carry

    lax.fori_loop(0, 4, grad_frame, 0)

    each_ctx(lambda peer: sums_copy(sums, sums_in, s_send, s_recv, peer).wait_send())
    each_ctx(lambda peer: sums_copy(sums2, sums2_in, s2_send, s2_recv, peer).wait_send())

    @pl.when(ctx < n_ctx - 1)
    def _():
        clip_halo.wait_send()

    @pl.when(ctx > 0)
    def _():
        edge_halo.wait_send()

    for chunk in range(3):
        pair_copy(chunk).wait_send()
    for quarter in range(4):
        for kind in (Y_FIRST, X_FIRST):
            for k in range(1, 4):
                first_step(quarter, kind, k).wait_send()
                second_step(quarter, kind, k).wait_send()
    for f in range(4):
        out_copy(f).wait()
        grad_copy(f).wait()
    for quarter in range(4):
        for to_lo in range(2):
            for to_core in range(2):
                mine = (z_hi == quarter) & (z_lo == to_lo) & (core == to_core)

                @pl.when(jnp.logical_not(mine))
                def _():
                    third_step(quarter, to_lo, to_core).wait_send()

    for from_z in range(8):
        for from_core in range(2):
            mine = (z_hi * 2 + z_lo == from_z) & (core == from_core)

            @pl.when(jnp.logical_not(mine))
            def _():
                third_arrival(from_z, from_core).wait_recv()

    halves = []
    for h in range(2):
        value = step3_in[0, h].astype(f32)
        for from_z in range(1, 8):
            value = value + step3_in[from_z, h].astype(f32)
        halves.append(value)
    value = jnp.concatenate(halves, axis=0) * (1.0 / (4 * n_ctx * n_dp))
    conv_buf[...] = value[:, 0:108]
    short_buf[...] = value.T[108:112]
    ends = [
        pltpu.make_async_copy(conv_buf, conv_grad, out_sem.at[8]),
        pltpu.make_async_copy(short_buf, short_grad, out_sem.at[9]),
    ]
    for copy in ends:
        copy.start()
    for copy in ends:
        copy.wait()


def store(*refs):
    sources, targets, sems = refs[0:4], refs[4:8], refs[8]
    copies = [pltpu.make_async_copy(sources[k], targets[k], sems.at[k]) for k in range(4)]
    for copy in copies:
        copy.start()
    for copy in copies:
        copy.wait()


def body(n_dp, n_ctx, clip_in, norm_gain, norm_bias, conv_weight, short_weight, out_cotangent):
    f32, bf16 = jnp.float32, jnp.bfloat16
    anywhere = pl.BlockSpec(memory_space=pl.ANY)
    hbm = pl.BlockSpec(memory_space=pltpu.HBM)
    dma = pltpu.SemaphoreType.DMA
    shapes = (
        jax.ShapeDtypeStruct((4, 384, 256), bf16),
        jax.ShapeDtypeStruct((4, 384, 128), bf16),
        jax.ShapeDtypeStruct((32, 108), f32),
        jax.ShapeDtypeStruct((4, 32), f32),
    )
    results = pl.pallas_call(
        functools.partial(kernel, n_dp, n_ctx),
        out_shape=shapes,
        in_specs=[hbm] * 6,
        out_specs=(anywhere,) * 4,
        scratch_shapes=[
            pltpu.VMEM((6, 384, 128), bf16),
            pltpu.VMEM((4, 576, 256), bf16),
            pltpu.VMEM((1, 128), f32),
            pltpu.VMEM((1, 128), f32),
            pltpu.VMEM((3584, 256), bf16),
            pltpu.VMEM((2304, 384), bf16),
            pltpu.VMEM((6, 576, 384), bf16),
            pltpu.VMEM((4, 384, 128), f32),
            pltpu.VMEM((2, 384, 128), bf16),
            pltpu.VMEM((2, 384, 128), bf16),
            pltpu.VMEM((256, 1536), bf16),
            pltpu.VMEM((2, 8, 128), f32),
            pltpu.VMEM((n_ctx, 2, 8, 128), f32),
            pltpu.VMEM((2, 8, 128), f32),
            pltpu.VMEM((n_ctx, 2, 8, 128), f32),
            pltpu.VMEM((3, n_ctx, 2, 16, 1280), f32),
            pltpu.VMEM((3, n_ctx, 16, 1280), f32),
            pltpu.VMEM((128, 3584), f32),
            pltpu.VMEM((4, 4, 32, 512), bf16),
            pltpu.VMEM((4, 4, 32, 512), bf16),
            pltpu.VMEM((4, 4, 128, 128), bf16),
            pltpu.VMEM((4, 4, 128, 128), bf16),
            pltpu.VMEM((4, 2, 4, 32, 128), f32),
            pltpu.VMEM((4, 2, 4, 32, 128), f32),
            pltpu.VMEM((4, 2, 2, 16, 128), f32),
            pltpu.VMEM((8, 2, 16, 128), f32),
            pltpu.VMEM((4, 384, 256), bf16),
            pltpu.VMEM((4, 384, 128), bf16),
            pltpu.VMEM((32, 108), f32),
            pltpu.VMEM((4, 32), f32),
            dma((6,)), dma((2,)), dma((2,)),
            dma((n_ctx,)), dma((n_ctx,)), dma((n_ctx,)), dma((n_ctx,)),
            dma((3,)), dma((3,)), dma((4, 2, 4)), dma((4, 2, 4)), dma((4, 2, 4)), dma((4, 2, 4)),
            dma((4, 2, 2)), dma((8, 2)), dma((10,)),
        ],
        compiler_params=pltpu.CompilerParams(
            collective_id=0, has_side_effects=True, vmem_limit_bytes=48 << 20
        ),
        name="conv_block",
    )(
        *[pltpu.with_memory_space_constraint(value, pltpu.HBM) for value in (
            clip_in.reshape(4, 384, 128), out_cotangent.reshape(4, 384, 256),
            norm_gain.reshape(1, 128), norm_bias.reshape(1, 128), conv_weight, short_weight,
        )]
    )
    out, grad, conv, short = pl.pallas_call(
        store,
        out_shape=shapes,
        in_specs=[anywhere] * 4,
        out_specs=(anywhere,) * 4,
        scratch_shapes=[dma((4,))],
        name="store",
    )(*[pltpu.with_memory_space_constraint(value, pltpu.VMEM) for value in results])
    return out.reshape(1, 4, 4, 96, 256), grad.reshape(1, 4, 4, 96, 128), conv.T, short


def solution(mesh):
    return jax.shard_map(
        functools.partial(body, mesh.shape["dp"], mesh.shape["ctx"]),
        mesh=mesh,
        in_specs=(
            P("dp", "ctx", None, None, None),
            P(),
            P(),
            P(),
            P(),
            P("dp", "ctx", None, None, None),
        ),
        out_specs=(
            P("dp", "ctx", None, None, None),
            P("dp", "ctx", None, None, None),
            P("dp", "ctx"),
            P("dp", "ctx"),
        ),
        check_vma=False,
    )
```

```python
import functools
import jax
import jax.numpy as jnp
from jax import lax
from jax.experimental import pallas as pl
from jax.experimental.pallas import tpu as pltpu
from jax.sharding import PartitionSpec as P

MESH = pl.DeviceIdType.MESH
GROUPS = 32
epsilon = 1e-06
TAPS = [(t, i) for t in range(3) for i in range(3)]
CHUNKS = ((2304, 1280), (1152, 1152), (0, 1152))
Y_FIRST, X_FIRST = 0, 1


def group_total(value):
    lane = lax.broadcasted_iota(jnp.int32, value.shape, 1)
    width = value.shape[1]
    value = value + jnp.where(lane % 2 == 0, pltpu.roll(value, width - 1, 1), pltpu.roll(value, 1, 1))
    return value + jnp.where(lane % 4 < 2, pltpu.roll(value, width - 2, 1), pltpu.roll(value, 2, 1))


def kernel(
    n_dp, n_ctx,
    clip, cot, gain, bias, conv_w, short_w,
    clip_out, clip_grad, conv_grad, short_grad,
    xall, cots, gain_buf, bias_buf, weight, weight_t, taps, back, edge, edge_in, cot_t,
    sums, sums_in, sums2, sums2_in,
    part, pair_in, total, y_out, y_in, x_out, x_in, step2, step2_in, step3, step3_in,
    out_buf, grad_buf, conv_buf, short_buf,
    in_sem, halo_send, halo_recv, s_send, s_recv, s2_send, s2_recv,
    pair_send, pair_recv, r1_send, r1_recv, r2_send, r2_recv, r3_send, r3_recv, out_sem,
):
    f32, bf16 = jnp.float32, jnp.bfloat16
    dp, ctx = lax.axis_index("dp"), lax.axis_index("ctx")
    z_hi, x, core = dp // 8, dp // 2 % 4, dp % 2
    y, z_lo = ctx // 2, ctx % 2
    members = 4 * n_ctx * 4 * 96 * 4

    def dp_of(z_hi, x, core):
        return (z_hi * 4 + x) * 2 + core

    def ctx_of(y, z_lo):
        return y * 2 + z_lo

    loads = [
        pltpu.make_async_copy(clip.at[0:2], xall.at[2:4], in_sem.at[0]),
        pltpu.make_async_copy(cot, cots.at[:, 96:480], in_sem.at[1]),
        pltpu.make_async_copy(conv_w, weight.at[0:3456], in_sem.at[2]),
        pltpu.make_async_copy(short_w, weight.at[3456:3584], in_sem.at[3]),
        pltpu.make_async_copy(gain, gain_buf, in_sem.at[4]),
        pltpu.make_async_copy(bias, bias_buf, in_sem.at[5]),
    ]
    late_clip = pltpu.make_async_copy(clip.at[2:4], xall.at[4:6], in_sem.at[6])
    late_clip.start()
    for copy in loads:
        copy.start()

    barrier = pltpu.get_barrier_semaphore()

    def greet(peer_dp, peer_ctx):
        pl.semaphore_signal(barrier, inc=1, device_id={"dp": peer_dp, "ctx": peer_ctx}, device_id_type=MESH)

    greetings = 0
    for k in range(1, n_ctx):
        greet(dp, (ctx + k) % n_ctx)
        greetings += 1
    for dz in range(4):
        for dl in range(2):
            for dc in range(2):
                if dz or dc:
                    greet(dp_of((z_hi + 4 - dz) % 4, x, (core + dc) % 2), ctx_of(y, (z_lo + dl) % 2))
                    greetings += 1
    for k in range(1, 4):
        greet(dp_of(z_hi, (x + k) % 4, core), ctx)
        greetings += 1

    loads[0].wait()
    first = jnp.zeros((8, 128), f32)
    second = jnp.zeros((8, 128), f32)
    for f in range(4):
        if f == 2:
            late_clip.wait()
        value = xall[2 + f].astype(f32).reshape(48, 8, 128)
        first = first + jnp.sum(value, axis=0)
        second = second + jnp.sum(value * value, axis=0)
    sums[0:1] = jnp.sum(first, axis=0, keepdims=True)
    sums[1:2] = jnp.sum(second, axis=0, keepdims=True)
    sums_in[ctx] = sums[...]

    pl.semaphore_wait(barrier, greetings)

    def sums_copy(source, target, send, recv, peer):
        return pltpu.make_async_remote_copy(
            src_ref=source, dst_ref=target.at[ctx], send_sem=send.at[peer], recv_sem=recv.at[ctx],
            device_id={"dp": dp, "ctx": peer}, device_id_type=MESH,
        )

    def sums_arrival(source, target, send, recv, peer):
        return pltpu.make_async_remote_copy(
            src_ref=source, dst_ref=target.at[peer], send_sem=send.at[peer], recv_sem=recv.at[peer],
            device_id={"dp": dp, "ctx": peer}, device_id_type=MESH,
        )

    def each_ctx(body):
        for k in range(1, n_ctx):
            body((ctx + k) % n_ctx)

    each_ctx(lambda peer: sums_copy(sums, sums_in, s_send, s_recv, peer).start())

    clip_halo = pltpu.make_async_remote_copy(
        src_ref=xall.at[4:6], dst_ref=xall.at[0:2], send_sem=halo_send.at[0], recv_sem=halo_recv.at[0],
        device_id={"dp": dp, "ctx": jnp.minimum(ctx + 1, n_ctx - 1)}, device_id_type=MESH,
    )
    edge_halo = pltpu.make_async_remote_copy(
        src_ref=edge, dst_ref=edge_in, send_sem=halo_send.at[1], recv_sem=halo_recv.at[1],
        device_id={"dp": dp, "ctx": jnp.maximum(ctx - 1, 0)}, device_id_type=MESH,
    )

    @pl.when(ctx < n_ctx - 1)
    def _():
        clip_halo.start()

    cots[:, 0:96] = jnp.zeros((4, 96, 256), bf16)
    cots[:, 480:576] = jnp.zeros((4, 96, 256), bf16)
    taps[:, 0:96] = jnp.zeros((6, 96, 384), bf16)
    taps[:, 480:576] = jnp.zeros((6, 96, 384), bf16)

    @pl.when(ctx == 0)
    def _():
        xall[0] = xall[2]
        xall[1] = xall[2]

    column = lax.broadcasted_iota(jnp.int32, (384, 128), 0) % 96
    at_left, at_right = column == 0, column == 95

    def from_left(value):
        return jnp.where(at_left, 0.0, pltpu.roll(value, 1, 0))

    def from_right(value):
        return jnp.where(at_right, 0.0, pltpu.roll(value, 383, 0))

    loads[1].wait()
    for f in range(4):
        cot_t[:, f * 384:f * 384 + 384] = cots[f, 96:480].T
    for copy in loads[2:]:
        copy.wait()
    for k in range(9):
        weight_t[k * 256:k * 256 + 256] = weight[k * 384:k * 384 + 384].T

    def back_terms(f, frame_taps):
        rows = jnp.concatenate(
            [cots[f + 2 - t, (2 - i) * 96:(2 - i) * 96 + 384] for t in frame_taps for i in range(3)], axis=1
        )
        turned = weight_t[frame_taps[0] * 768:frame_taps[-1] * 768 + 768]
        product = jnp.dot(rows, turned, preferred_element_type=f32)
        return from_right(product[:, 0:128]) + product[:, 128:256] + from_left(product[:, 256:384])

    ahead = back_terms(-2, (0,)), back_terms(-1, (0, 1))
    back[0] = back_terms(0, (0, 1, 2))

    @pl.when(ctx == 0)
    def _():
        back[0] = back[0] + (ahead[0] + ahead[1])

    edge[0] = ahead[0].astype(bf16)
    edge[1] = ahead[1].astype(bf16)

    @pl.when(ctx > 0)
    def _():
        edge_halo.start()

    back[1] = back_terms(1, (0, 1, 2))

    each_ctx(lambda peer: sums_arrival(sums, sums_in, s_send, s_recv, peer).wait_recv())
    all_sums = jnp.sum(sums_in[...], axis=0)
    all_sums = group_total(jnp.concatenate([all_sums, jnp.zeros((6, 128), f32)], axis=0))
    mean = all_sums[0:1] / members
    variance = all_sums[1:2] / members - mean * mean
    inv = lax.rsqrt(variance + epsilon)
    gain_row, bias_row = gain_buf[...], bias_buf[...]

    def standard_of(f):
        return (xall[f].astype(f32) - mean) * inv

    def hidden_frame(f, carry):
        affine = standard_of(f) * gain_row + bias_row
        hidden = affine * jax.nn.sigmoid(affine)
        taps[f, 96:480, 0:128] = from_left(hidden).astype(bf16)
        taps[f, 96:480, 128:256] = hidden.astype(bf16)
        taps[f, 96:480, 256:384] = from_right(hidden).astype(bf16)
        return carry

    lax.fori_loop(2, 6, hidden_frame, 0)

    def pair_copy(chunk):
        lanes = pl.ds(0, CHUNKS[chunk][1])
        return pltpu.make_async_remote_copy(
            src_ref=part.at[chunk, :, 1 - core, :, lanes], dst_ref=pair_in.at[chunk, :, :, lanes],
            send_sem=pair_send.at[chunk], recv_sem=pair_recv.at[chunk],
            device_id={"dp": dp + 1 - 2 * core, "ctx": ctx}, device_id_type=MESH,
        )

    def multiply(chunk):
        t = 2 - chunk
        columns = [
            jnp.concatenate([taps[f + t, i * 96:i * 96 + 384] for f in range(4)], axis=0) for i in range(3)
        ]
        if chunk == 0:
            columns.append(jnp.concatenate([xall[2 + f] for f in range(4)], axis=0))
        width = CHUNKS[chunk][1]
        product = jnp.dot(cot_t[...], jnp.concatenate(columns, axis=1), preferred_element_type=f32)
        part[chunk, :, :, :, 0:width] = product.reshape(n_ctx, 2, 16, width)
        pair_copy(chunk).start()

    def add_pair(chunk):
        start, width = CHUNKS[chunk]
        pair_copy(chunk).wait_recv()
        value = part[chunk, :, core, :, 0:width] + pair_in[chunk, :, :, 0:width]
        total[:, start:start + width] = value.reshape(n_ctx * 16, width)

    def peer_at(along_y, k):
        if along_y:
            place = (y + k) % 4
            return place, {"dp": dp, "ctx": ctx_of(place, z_lo)}
        place = (x + k) % 4
        return place, {"dp": dp_of(z_hi, place, core), "ctx": ctx}

    def first_step(quarter, kind, k, arriving=False):
        along_y = kind == Y_FIRST
        source, target = (y_out, y_in) if along_y else (x_out, x_in)
        place, device = peer_at(along_y, k)
        slot = place if arriving else (y if along_y else x)
        return pltpu.make_async_remote_copy(
            src_ref=source.at[quarter, place], dst_ref=target.at[quarter, slot],
            send_sem=r1_send.at[quarter, kind, place], recv_sem=r1_recv.at[quarter, kind, slot],
            device_id=device, device_id_type=MESH,
        )

    def second_step(quarter, kind, k, arriving=False):
        along_y = kind == X_FIRST
        place, device = peer_at(along_y, k)
        slot = place if arriving else (y if along_y else x)
        return pltpu.make_async_remote_copy(
            src_ref=step2.at[quarter, kind, place], dst_ref=step2_in.at[quarter, kind, slot],
            send_sem=r2_send.at[quarter, kind, place], recv_sem=r2_recv.at[quarter, kind, slot],
            device_id=device, device_id_type=MESH,
        )

    def third_step(quarter, to_lo, to_core):
        return pltpu.make_async_remote_copy(
            src_ref=step3.at[quarter, to_lo, to_core], dst_ref=step3_in.at[z_hi * 2 + z_lo, core],
            send_sem=r3_send.at[quarter, to_lo, to_core], recv_sem=r3_recv.at[z_hi * 2 + z_lo, core],
            device_id={"dp": dp_of(quarter, x, to_core), "ctx": ctx_of(y, to_lo)}, device_id_type=MESH,
        )

    def third_arrival(from_z, from_core):
        return pltpu.make_async_remote_copy(
            src_ref=step3.at[0, 0, 0], dst_ref=step3_in.at[from_z, from_core],
            send_sem=r3_send.at[0, 0, 0], recv_sem=r3_recv.at[from_z, from_core],
            device_id={"dp": dp_of(from_z // 2, x, from_core), "ctx": ctx_of(y, from_z % 2)}, device_id_type=MESH,
        )

    lane = lax.broadcasted_iota(jnp.int32, (128, 128), 1)

    def begin(quarter):
        short_lanes = total[:, 3456:3584]
        for place in range(8):
            owner = 8 * quarter + place
            base = 108 * owner // 128 * 128
            shift = 108 * owner - base
            value = total[:, base:base + 256]
            if shift:
                value = pltpu.roll(value, 256 - shift, 1)
            tail = (108 - 4 * owner) % 128
            tail = pltpu.roll(short_lanes, tail, 1) if tail else short_lanes
            value = jnp.where(lane < 108, value[:, 0:128], tail).astype(bf16)
            if place % 2 == Y_FIRST:
                at = place // 2 * 128
                y_out[quarter, :, :, at:at + 128] = value.reshape(4, 32, 128)
            else:
                x_out[quarter, place // 2] = value
        for k in (2, 1, 3):
            first_step(quarter, Y_FIRST, k).start()
            first_step(quarter, X_FIRST, k).start()
        y_in[quarter, y] = y_out[quarter, y]
        x_in[quarter, x] = x_out[quarter, x]

    def go_on(quarter):
        for kind, arrived in ((Y_FIRST, y_in), (X_FIRST, x_in)):
            for k in (1, 3, 2):
                first_step(quarter, kind, k, arriving=True).wait_recv()
            value = arrived[quarter, 0].astype(f32)
            for place in range(1, 4):
                value = value + arrived[quarter, place].astype(f32)
            if kind == Y_FIRST:
                for place in range(4):
                    step2[quarter, kind, place] = value[:, place * 128:place * 128 + 128]
            else:
                step2[quarter, kind] = value.reshape(4, 32, 128)
            for k in (2, 1, 3):
                second_step(quarter, kind, k).start()
            own = x if kind == Y_FIRST else y
            step2_in[quarter, kind, own] = step2[quarter, kind, own]

    def finish(quarter):
        for kind in (Y_FIRST, X_FIRST):
            to_core = kind
            for k in (1, 3, 2):
                second_step(quarter, kind, k, arriving=True).wait_recv()
            value = step2_in[quarter, kind, 0]
            for place in range(1, 4):
                value = value + step2_in[quarter, kind, place]
            value = value.astype(step3.dtype)
            for to_lo in range(2):
                step3[quarter, to_lo, to_core] = value[to_lo * 16:to_lo * 16 + 16]
                mine = (z_hi == quarter) & (z_lo == to_lo) & (core == to_core)

                @pl.when(jnp.logical_not(mine))
                def _():
                    third_step(quarter, to_lo, to_core).start()

                @pl.when(mine)
                def _():
                    step3_in[z_hi * 2 + z_lo, core] = step3[quarter, to_lo, to_core]

    multiply(0)

    @pl.when(ctx > 0)
    def _():
        clip_halo.wait_recv()

    lax.fori_loop(0, 2, hidden_frame, 0)
    multiply(1)
    add_pair(0)
    begin(3)
    multiply(2)
    add_pair(1)
    begin(2)
    back[2] = back_terms(2, (1, 2))
    add_pair(2)
    begin(1)
    begin(0)

    back[3] = back_terms(3, (2,))

    @pl.when(ctx < n_ctx - 1)
    def _():
        edge_halo.wait_recv()
        back[2] = back[2] + edge_in[0].astype(f32)
        back[3] = back[3] + edge_in[1].astype(f32)

    def norm_frame(f, carry):
        standard = standard_of(f + 2)
        affine = standard * gain_row + bias_row
        logistic = jax.nn.sigmoid(affine)
        grad = back[f] * logistic * (1.0 + affine * (1.0 - logistic)) * gain_row
        back[f] = grad
        return (
            carry[0] + jnp.sum(grad.reshape(48, 8, 128), axis=0),
            carry[1] + jnp.sum((grad * standard).reshape(48, 8, 128), axis=0),
        )

    zero = jnp.zeros((8, 128), f32)
    grad_sum, cross_sum = lax.fori_loop(0, 4, norm_frame, (zero, zero))
    sums2[0:1] = jnp.sum(grad_sum, axis=0, keepdims=True)
    sums2[1:2] = jnp.sum(cross_sum, axis=0, keepdims=True)
    sums2_in[ctx] = sums2[...]
    each_ctx(lambda peer: sums_copy(sums2, sums2_in, s2_send, s2_recv, peer).start())

    def out_copy(f):
        return pltpu.make_async_copy(out_buf.at[f], clip_out.at[f], out_sem.at[f])

    def grad_copy(f):
        return pltpu.make_async_copy(grad_buf.at[f], clip_grad.at[f], out_sem.at[4 + f])

    def out_frame(f, carry):
        rows = jnp.concatenate([taps[f + t, i * 96:i * 96 + 384] for t, i in TAPS] + [xall[f + 2]], axis=1)
        out_buf[f] = jnp.dot(rows, weight[...], preferred_element_type=f32).astype(bf16)
        out_copy(f).start()
        return carry

    go_on(3)
    go_on(2)
    lax.fori_loop(0, 2, out_frame, 0)
    go_on(1)
    go_on(0)
    finish(3)
    finish(2)
    lax.fori_loop(2, 3, out_frame, 0)
    finish(1)
    finish(0)
    lax.fori_loop(3, 4, out_frame, 0)

    each_ctx(lambda peer: sums_arrival(sums2, sums2_in, s2_send, s2_recv, peer).wait_recv())
    all_sums = jnp.sum(sums2_in[...], axis=0)
    all_sums = group_total(jnp.concatenate([all_sums, jnp.zeros((6, 128), f32)], axis=0)) / members
    mean_grad, mean_cross = all_sums[0:1], all_sums[1:2]

    def grad_frame(f, carry):
        shortcut = lax.dot_general(
            cots[f, 96:480], weight[3456:3584], (((1,), (1,)), ((), ())), preferred_element_type=f32
        )
        value = (back[f] - mean_grad - standard_of(f + 2) * mean_cross) * inv + shortcut
        grad_buf[f] = value.astype(bf16)
        grad_copy(f).start()
        return carry

    lax.fori_loop(0, 4, grad_frame, 0)

    each_ctx(lambda peer: sums_copy(sums, sums_in, s_send, s_recv, peer).wait_send())
    each_ctx(lambda peer: sums_copy(sums2, sums2_in, s2_send, s2_recv, peer).wait_send())

    @pl.when(ctx < n_ctx - 1)
    def _():
        clip_halo.wait_send()

    @pl.when(ctx > 0)
    def _():
        edge_halo.wait_send()

    for chunk in range(3):
        pair_copy(chunk).wait_send()
    for quarter in range(4):
        for kind in (Y_FIRST, X_FIRST):
            for k in range(1, 4):
                first_step(quarter, kind, k).wait_send()
                second_step(quarter, kind, k).wait_send()
    for f in range(4):
        out_copy(f).wait()
        grad_copy(f).wait()
    for quarter in range(4):
        for to_lo in range(2):
            for to_core in range(2):
                mine = (z_hi == quarter) & (z_lo == to_lo) & (core == to_core)

                @pl.when(jnp.logical_not(mine))
                def _():
                    third_step(quarter, to_lo, to_core).wait_send()

    for from_z in range(8):
        for from_core in range(2):
            mine = (z_hi * 2 + z_lo == from_z) & (core == from_core)

            @pl.when(jnp.logical_not(mine))
            def _():
                third_arrival(from_z, from_core).wait_recv()

    halves = []
    for h in range(2):
        value = step3_in[0, h].astype(f32)
        for from_z in range(1, 8):
            value = value + step3_in[from_z, h].astype(f32)
        halves.append(value)
    value = jnp.concatenate(halves, axis=0) * (1.0 / (4 * n_ctx * n_dp))
    conv_buf[...] = value[:, 0:108]
    short_buf[...] = value.T[108:112]
    ends = [
        pltpu.make_async_copy(conv_buf, conv_grad, out_sem.at[8]),
        pltpu.make_async_copy(short_buf, short_grad, out_sem.at[9]),
    ]
    for copy in ends:
        copy.start()
    for copy in ends:
        copy.wait()


def store(*refs):
    sources, targets, sems = refs[0:4], refs[4:8], refs[8]
    pairs = [(sources[k].at[f], targets[k].at[f]) for k in range(2) for f in range(4)]
    pairs += [(sources[k], targets[k]) for k in range(2, 4)]
    copies = [pltpu.make_async_copy(source, target, sems.at[k]) for k, (source, target) in enumerate(pairs)]
    for copy in copies:
        copy.start()
    for copy in copies:
        copy.wait()


def body(n_dp, n_ctx, clip_in, norm_gain, norm_bias, conv_weight, short_weight, out_cotangent):
    f32, bf16 = jnp.float32, jnp.bfloat16
    anywhere = pl.BlockSpec(memory_space=pl.ANY)
    hbm = pl.BlockSpec(memory_space=pltpu.HBM)
    dma = pltpu.SemaphoreType.DMA
    shapes = (
        jax.ShapeDtypeStruct((4, 384, 256), bf16),
        jax.ShapeDtypeStruct((4, 384, 128), bf16),
        jax.ShapeDtypeStruct((32, 108), f32),
        jax.ShapeDtypeStruct((4, 32), f32),
    )
    results = pl.pallas_call(
        functools.partial(kernel, n_dp, n_ctx),
        out_shape=shapes,
        in_specs=[hbm] * 6,
        out_specs=(anywhere,) * 4,
        scratch_shapes=[
            pltpu.VMEM((6, 384, 128), bf16),
            pltpu.VMEM((4, 576, 256), bf16),
            pltpu.VMEM((1, 128), f32),
            pltpu.VMEM((1, 128), f32),
            pltpu.VMEM((3584, 256), bf16),
            pltpu.VMEM((2304, 384), bf16),
            pltpu.VMEM((6, 576, 384), bf16),
            pltpu.VMEM((4, 384, 128), f32),
            pltpu.VMEM((2, 384, 128), bf16),
            pltpu.VMEM((2, 384, 128), bf16),
            pltpu.VMEM((256, 1536), bf16),
            pltpu.VMEM((2, 128), f32),
            pltpu.VMEM((n_ctx, 2, 128), f32),
            pltpu.VMEM((2, 128), f32),
            pltpu.VMEM((n_ctx, 2, 128), f32),
            pltpu.VMEM((3, n_ctx, 2, 16, 1280), f32),
            pltpu.VMEM((3, n_ctx, 16, 1280), f32),
            pltpu.VMEM((128, 3584), f32),
            pltpu.VMEM((4, 4, 32, 512), bf16),
            pltpu.VMEM((4, 4, 32, 512), bf16),
            pltpu.VMEM((4, 4, 128, 128), bf16),
            pltpu.VMEM((4, 4, 128, 128), bf16),
            pltpu.VMEM((4, 2, 4, 32, 128), f32),
            pltpu.VMEM((4, 2, 4, 32, 128), f32),
            pltpu.VMEM((4, 2, 2, 16, 128), f32),
            pltpu.VMEM((8, 2, 16, 128), f32),
            pltpu.VMEM((4, 384, 256), bf16),
            pltpu.VMEM((4, 384, 128), bf16),
            pltpu.VMEM((32, 108), f32),
            pltpu.VMEM((4, 32), f32),
            dma((7,)), dma((2,)), dma((2,)),
            dma((n_ctx,)), dma((n_ctx,)), dma((n_ctx,)), dma((n_ctx,)),
            dma((3,)), dma((3,)), dma((4, 2, 4)), dma((4, 2, 4)), dma((4, 2, 4)), dma((4, 2, 4)),
            dma((4, 2, 2)), dma((8, 2)), dma((10,)),
        ],
        compiler_params=pltpu.CompilerParams(
            collective_id=0, has_side_effects=True, vmem_limit_bytes=48 << 20
        ),
        name="conv_block",
    )(
        *[pltpu.with_memory_space_constraint(value, pltpu.HBM) for value in (
            clip_in.reshape(4, 384, 128), out_cotangent.reshape(4, 384, 256),
            norm_gain.reshape(1, 128), norm_bias.reshape(1, 128), conv_weight, short_weight,
        )]
    )
    out, grad, conv, short = pl.pallas_call(
        store,
        out_shape=shapes,
        in_specs=[anywhere] * 4,
        out_specs=(anywhere,) * 4,
        scratch_shapes=[dma((10,))],
        name="store",
    )(*[pltpu.with_memory_space_constraint(value, pltpu.VMEM) for value in results])
    return out.reshape(1, 4, 4, 96, 256), grad.reshape(1, 4, 4, 96, 128), conv.T, short


def solution(mesh):
    return jax.shard_map(
        functools.partial(body, mesh.shape["dp"], mesh.shape["ctx"]),
        mesh=mesh,
        in_specs=(
            P("dp", "ctx", None, None, None),
            P(),
            P(),
            P(),
            P(),
            P("dp", "ctx", None, None, None),
        ),
        out_specs=(
            P("dp", "ctx", None, None, None),
            P("dp", "ctx", None, None, None),
            P("dp", "ctx"),
            P("dp", "ctx"),
        ),
        check_vma=False,
    )
```

```python
import functools
import jax
import jax.numpy as jnp
from jax import lax
from jax.experimental import pallas as pl
from jax.experimental.pallas import tpu as pltpu
from jax.sharding import PartitionSpec as P

MESH = pl.DeviceIdType.MESH
GROUPS = 32
epsilon = 1e-06
TAPS = [(t, i) for t in range(3) for i in range(3)]
CHUNKS = ((2304, 1280), (1152, 1152), (0, 1152))
Y_FIRST, X_FIRST = 0, 1


def group_total(value):
    lane = lax.broadcasted_iota(jnp.int32, value.shape, 1)
    width = value.shape[1]
    value = value + jnp.where(lane % 2 == 0, pltpu.roll(value, width - 1, 1), pltpu.roll(value, 1, 1))
    return value + jnp.where(lane % 4 < 2, pltpu.roll(value, width - 2, 1), pltpu.roll(value, 2, 1))


def kernel(
    n_dp, n_ctx,
    clip, cot, gain, bias, conv_w, short_w,
    clip_out, clip_grad, conv_grad, short_grad,
    xall, cots, gain_buf, bias_buf, weight, weight_t, taps, back, edge, edge_in, cot_t,
    sums, sums_in, sums2, sums2_in,
    part, pair_in, total, y_out, y_in, x_out, x_in, step2, step2_in, step3, step3_in,
    out_buf, grad_buf, conv_buf, short_buf,
    in_sem, halo_send, halo_recv, s_send, s_recv, s2_send, s2_recv,
    pair_send, pair_recv, r1_send, r1_recv, r2_send, r2_recv, r3_send, r3_recv, out_sem,
):
    f32, bf16 = jnp.float32, jnp.bfloat16
    dp, ctx = lax.axis_index("dp"), lax.axis_index("ctx")
    z_hi, x, core = dp // 8, dp // 2 % 4, dp % 2
    y, z_lo = ctx // 2, ctx % 2
    members = 4 * n_ctx * 4 * 96 * 4

    def dp_of(z_hi, x, core):
        return (z_hi * 4 + x) * 2 + core

    def ctx_of(y, z_lo):
        return y * 2 + z_lo

    loads = [
        pltpu.make_async_copy(clip.at[0:2], xall.at[2:4], in_sem.at[0]),
        pltpu.make_async_copy(cot, cots.at[:, 96:480], in_sem.at[1]),
        pltpu.make_async_copy(conv_w, weight.at[0:3456], in_sem.at[2]),
        pltpu.make_async_copy(short_w, weight.at[3456:3584], in_sem.at[3]),
        pltpu.make_async_copy(gain, gain_buf, in_sem.at[4]),
        pltpu.make_async_copy(bias, bias_buf, in_sem.at[5]),
    ]
    late_clip = pltpu.make_async_copy(clip.at[2:4], xall.at[4:6], in_sem.at[6])
    late_clip.start()
    for copy in loads:
        copy.start()

    barrier = pltpu.get_barrier_semaphore()

    def greet(peer_dp, peer_ctx):
        pl.semaphore_signal(barrier, inc=1, device_id={"dp": peer_dp, "ctx": peer_ctx}, device_id_type=MESH)

    greetings = 0
    for k in range(1, n_ctx):
        greet(dp, (ctx + k) % n_ctx)
        greetings += 1
    for dz in range(4):
        for dl in range(2):
            for dc in range(2):
                if dz or dc:
                    greet(dp_of((z_hi + 4 - dz) % 4, x, (core + dc) % 2), ctx_of(y, (z_lo + dl) % 2))
                    greetings += 1
    for k in range(1, 4):
        greet(dp_of(z_hi, (x + k) % 4, core), ctx)
        greetings += 1

    loads[0].wait()
    first = jnp.zeros((8, 128), f32)
    second = jnp.zeros((8, 128), f32)
    for f in range(4):
        if f == 2:
            late_clip.wait()
        value = xall[2 + f].astype(f32).reshape(48, 8, 128)
        first = first + jnp.sum(value, axis=0)
        second = second + jnp.sum(value * value, axis=0)
    sums[0:1] = jnp.sum(first, axis=0, keepdims=True)
    sums[1:2] = jnp.sum(second, axis=0, keepdims=True)
    sums_in[ctx] = sums[...]

    pl.semaphore_wait(barrier, greetings)

    def sums_copy(source, target, send, recv, peer):
        return pltpu.make_async_remote_copy(
            src_ref=source, dst_ref=target.at[ctx], send_sem=send.at[peer], recv_sem=recv.at[ctx],
            device_id={"dp": dp, "ctx": peer}, device_id_type=MESH,
        )

    def sums_arrival(source, target, send, recv, peer):
        return pltpu.make_async_remote_copy(
            src_ref=source, dst_ref=target.at[peer], send_sem=send.at[peer], recv_sem=recv.at[peer],
            device_id={"dp": dp, "ctx": peer}, device_id_type=MESH,
        )

    def each_ctx(body):
        for k in range(1, n_ctx):
            body((ctx + k) % n_ctx)

    each_ctx(lambda peer: sums_copy(sums, sums_in, s_send, s_recv, peer).start())

    clip_halo = pltpu.make_async_remote_copy(
        src_ref=xall.at[4:6], dst_ref=xall.at[0:2], send_sem=halo_send.at[0], recv_sem=halo_recv.at[0],
        device_id={"dp": dp, "ctx": jnp.minimum(ctx + 1, n_ctx - 1)}, device_id_type=MESH,
    )
    edge_halo = pltpu.make_async_remote_copy(
        src_ref=edge, dst_ref=edge_in, send_sem=halo_send.at[1], recv_sem=halo_recv.at[1],
        device_id={"dp": dp, "ctx": jnp.maximum(ctx - 1, 0)}, device_id_type=MESH,
    )

    @pl.when(ctx < n_ctx - 1)
    def _():
        clip_halo.start()

    cots[:, 0:96] = jnp.zeros((4, 96, 256), bf16)
    cots[:, 480:576] = jnp.zeros((4, 96, 256), bf16)
    taps[:, 0:96] = jnp.zeros((6, 96, 384), bf16)
    taps[:, 480:576] = jnp.zeros((6, 96, 384), bf16)

    @pl.when(ctx == 0)
    def _():
        xall[0] = xall[2]
        xall[1] = xall[2]

    column = lax.broadcasted_iota(jnp.int32, (384, 128), 0) % 96
    at_left, at_right = column == 0, column == 95

    def from_left(value):
        return jnp.where(at_left, 0.0, pltpu.roll(value, 1, 0))

    def from_right(value):
        return jnp.where(at_right, 0.0, pltpu.roll(value, 383, 0))

    loads[1].wait()
    for f in range(4):
        cot_t[:, f * 384:f * 384 + 384] = cots[f, 96:480].T
    for copy in loads[2:]:
        copy.wait()
    for k in range(9):
        weight_t[k * 256:k * 256 + 256] = weight[k * 384:k * 384 + 384].T

    def back_terms(f, frame_taps):
        rows = jnp.concatenate(
            [cots[f + 2 - t, (2 - i) * 96:(2 - i) * 96 + 384] for t in frame_taps for i in range(3)], axis=1
        )
        turned = weight_t[frame_taps[0] * 768:frame_taps[-1] * 768 + 768]
        product = jnp.dot(rows, turned, preferred_element_type=f32)
        return from_right(product[:, 0:128]) + product[:, 128:256] + from_left(product[:, 256:384])

    ahead = back_terms(-2, (0,)), back_terms(-1, (0, 1))
    back[0] = back_terms(0, (0, 1, 2))

    @pl.when(ctx == 0)
    def _():
        back[0] = back[0] + (ahead[0] + ahead[1])

    edge[0] = ahead[0].astype(bf16)
    edge[1] = ahead[1].astype(bf16)

    @pl.when(ctx > 0)
    def _():
        edge_halo.start()

    each_ctx(lambda peer: sums_arrival(sums, sums_in, s_send, s_recv, peer).wait_recv())
    all_sums = jnp.sum(sums_in[...], axis=0)
    all_sums = group_total(jnp.concatenate([all_sums, jnp.zeros((6, 128), f32)], axis=0))
    mean = all_sums[0:1] / members
    variance = all_sums[1:2] / members - mean * mean
    inv = lax.rsqrt(variance + epsilon)
    gain_row, bias_row = gain_buf[...], bias_buf[...]

    def standard_of(f):
        return (xall[f].astype(f32) - mean) * inv

    def hidden_frame(f, carry):
        affine = standard_of(f) * gain_row + bias_row
        hidden = affine * jax.nn.sigmoid(affine)
        taps[f, 96:480, 0:128] = from_left(hidden).astype(bf16)
        taps[f, 96:480, 128:256] = hidden.astype(bf16)
        taps[f, 96:480, 256:384] = from_right(hidden).astype(bf16)
        return carry

    lax.fori_loop(2, 6, hidden_frame, 0)

    def pair_copy(chunk):
        lanes = pl.ds(0, CHUNKS[chunk][1])
        return pltpu.make_async_remote_copy(
            src_ref=part.at[chunk, :, 1 - core, :, lanes], dst_ref=pair_in.at[chunk, :, :, lanes],
            send_sem=pair_send.at[chunk], recv_sem=pair_recv.at[chunk],
            device_id={"dp": dp + 1 - 2 * core, "ctx": ctx}, device_id_type=MESH,
        )

    def multiply(chunk):
        t = 2 - chunk
        columns = [
            jnp.concatenate([taps[f + t, i * 96:i * 96 + 384] for f in range(4)], axis=0) for i in range(3)
        ]
        if chunk == 0:
            columns.append(jnp.concatenate([xall[2 + f] for f in range(4)], axis=0))
        width = CHUNKS[chunk][1]
        product = jnp.dot(cot_t[...], jnp.concatenate(columns, axis=1), preferred_element_type=f32)
        part[chunk, :, :, :, 0:width] = product.reshape(n_ctx, 2, 16, width)
        pair_copy(chunk).start()

    def add_pair(chunk):
        start, width = CHUNKS[chunk]
        pair_copy(chunk).wait_recv()
        value = part[chunk, :, core, :, 0:width] + pair_in[chunk, :, :, 0:width]
        total[:, start:start + width] = value.reshape(n_ctx * 16, width)

    def peer_at(along_y, k):
        if along_y:
            place = (y + k) % 4
            return place, {"dp": dp, "ctx": ctx_of(place, z_lo)}
        place = (x + k) % 4
        return place, {"dp": dp_of(z_hi, place, core), "ctx": ctx}

    def first_step(quarter, kind, k, arriving=False):
        along_y = kind == Y_FIRST
        source, target = (y_out, y_in) if along_y else (x_out, x_in)
        place, device = peer_at(along_y, k)
        slot = place if arriving else (y if along_y else x)
        return pltpu.make_async_remote_copy(
            src_ref=source.at[quarter, place], dst_ref=target.at[quarter, slot],
            send_sem=r1_send.at[quarter, kind, place], recv_sem=r1_recv.at[quarter, kind, slot],
            device_id=device, device_id_type=MESH,
        )

    def second_step(quarter, kind, k, arriving=False):
        along_y = kind == X_FIRST
        place, device = peer_at(along_y, k)
        slot = place if arriving else (y if along_y else x)
        return pltpu.make_async_remote_copy(
            src_ref=step2.at[quarter, kind, place], dst_ref=step2_in.at[quarter, kind, slot],
            send_sem=r2_send.at[quarter, kind, place], recv_sem=r2_recv.at[quarter, kind, slot],
            device_id=device, device_id_type=MESH,
        )

    def third_step(quarter, to_lo, to_core):
        return pltpu.make_async_remote_copy(
            src_ref=step3.at[quarter, to_lo, to_core], dst_ref=step3_in.at[z_hi * 2 + z_lo, core],
            send_sem=r3_send.at[quarter, to_lo, to_core], recv_sem=r3_recv.at[z_hi * 2 + z_lo, core],
            device_id={"dp": dp_of(quarter, x, to_core), "ctx": ctx_of(y, to_lo)}, device_id_type=MESH,
        )

    def third_arrival(from_z, from_core):
        return pltpu.make_async_remote_copy(
            src_ref=step3.at[0, 0, 0], dst_ref=step3_in.at[from_z, from_core],
            send_sem=r3_send.at[0, 0, 0], recv_sem=r3_recv.at[from_z, from_core],
            device_id={"dp": dp_of(from_z // 2, x, from_core), "ctx": ctx_of(y, from_z % 2)}, device_id_type=MESH,
        )

    lane = lax.broadcasted_iota(jnp.int32, (128, 128), 1)

    def begin(quarter):
        short_lanes = total[:, 3456:3584]
        for place in range(8):
            owner = 8 * quarter + place
            base = 108 * owner // 128 * 128
            shift = 108 * owner - base
            value = total[:, base:base + 256]
            if shift:
                value = pltpu.roll(value, 256 - shift, 1)
            tail = (108 - 4 * owner) % 128
            tail = pltpu.roll(short_lanes, tail, 1) if tail else short_lanes
            value = jnp.where(lane < 108, value[:, 0:128], tail).astype(bf16)
            if place % 2 == Y_FIRST:
                at = place // 2 * 128
                y_out[quarter, :, :, at:at + 128] = value.reshape(4, 32, 128)
            else:
                x_out[quarter, place // 2] = value
        for k in (2, 1, 3):
            first_step(quarter, Y_FIRST, k).start()
            first_step(quarter, X_FIRST, k).start()
        y_in[quarter, y] = y_out[quarter, y]
        x_in[quarter, x] = x_out[quarter, x]

    def go_on(quarter):
        for kind, arrived in ((Y_FIRST, y_in), (X_FIRST, x_in)):
            for k in (1, 3, 2):
                first_step(quarter, kind, k, arriving=True).wait_recv()
            value = arrived[quarter, 0].astype(f32)
            for place in range(1, 4):
                value = value + arrived[quarter, place].astype(f32)
            if kind == Y_FIRST:
                for place in range(4):
                    step2[quarter, kind, place] = value[:, place * 128:place * 128 + 128]
            else:
                step2[quarter, kind] = value.reshape(4, 32, 128)
            for k in (2, 1, 3):
                second_step(quarter, kind, k).start()
            own = x if kind == Y_FIRST else y
            step2_in[quarter, kind, own] = step2[quarter, kind, own]

    def finish(quarter):
        for kind in (Y_FIRST, X_FIRST):
            to_core = kind
            for k in (1, 3, 2):
                second_step(quarter, kind, k, arriving=True).wait_recv()
            value = step2_in[quarter, kind, 0]
            for place in range(1, 4):
                value = value + step2_in[quarter, kind, place]
            value = value.astype(step3.dtype)
            for to_lo in range(2):
                step3[quarter, to_lo, to_core] = value[to_lo * 16:to_lo * 16 + 16]
                mine = (z_hi == quarter) & (z_lo == to_lo) & (core == to_core)

                @pl.when(jnp.logical_not(mine))
                def _():
                    third_step(quarter, to_lo, to_core).start()

                @pl.when(mine)
                def _():
                    step3_in[z_hi * 2 + z_lo, core] = step3[quarter, to_lo, to_core]

    multiply(0)

    @pl.when(ctx > 0)
    def _():
        clip_halo.wait_recv()

    lax.fori_loop(0, 2, hidden_frame, 0)
    multiply(1)
    add_pair(0)
    begin(3)
    multiply(2)
    add_pair(1)
    begin(2)
    back[2] = back_terms(2, (1, 2))
    add_pair(2)
    begin(1)
    begin(0)

    back[3] = back_terms(3, (2,))
    back[1] = back_terms(1, (0, 1, 2))

    @pl.when(ctx < n_ctx - 1)
    def _():
        edge_halo.wait_recv()
        back[2] = back[2] + edge_in[0].astype(f32)
        back[3] = back[3] + edge_in[1].astype(f32)

    def norm_frame(f, carry):
        standard = standard_of(f + 2)
        affine = standard * gain_row + bias_row
        logistic = jax.nn.sigmoid(affine)
        grad = back[f] * logistic * (1.0 + affine * (1.0 - logistic)) * gain_row
        back[f] = grad
        return (
            carry[0] + jnp.sum(grad.reshape(48, 8, 128), axis=0),
            carry[1] + jnp.sum((grad * standard).reshape(48, 8, 128), axis=0),
        )

    zero = jnp.zeros((8, 128), f32)
    grad_sum, cross_sum = lax.fori_loop(0, 4, norm_frame, (zero, zero))
    sums2[0:1] = jnp.sum(grad_sum, axis=0, keepdims=True)
    sums2[1:2] = jnp.sum(cross_sum, axis=0, keepdims=True)
    sums2_in[ctx] = sums2[...]
    each_ctx(lambda peer: sums_copy(sums2, sums2_in, s2_send, s2_recv, peer).start())

    def out_copy(f):
        return pltpu.make_async_copy(out_buf.at[f], clip_out.at[f], out_sem.at[f])

    def grad_copy(f):
        return pltpu.make_async_copy(grad_buf.at[f], clip_grad.at[f], out_sem.at[4 + f])

    def out_frame(f, carry):
        rows = jnp.concatenate([taps[f + t, i * 96:i * 96 + 384] for t, i in TAPS] + [xall[f + 2]], axis=1)
        out_buf[f] = jnp.dot(rows, weight[...], preferred_element_type=f32).astype(bf16)
        out_copy(f).start()
        return carry

    go_on(3)
    go_on(2)
    lax.fori_loop(0, 2, out_frame, 0)
    go_on(1)
    go_on(0)
    finish(3)
    finish(2)
    lax.fori_loop(2, 3, out_frame, 0)
    finish(1)
    finish(0)
    lax.fori_loop(3, 4, out_frame, 0)

    each_ctx(lambda peer: sums_arrival(sums2, sums2_in, s2_send, s2_recv, peer).wait_recv())
    all_sums = jnp.sum(sums2_in[...], axis=0)
    all_sums = group_total(jnp.concatenate([all_sums, jnp.zeros((6, 128), f32)], axis=0)) / members
    mean_grad, mean_cross = all_sums[0:1], all_sums[1:2]

    def grad_frame(f, carry):
        shortcut = lax.dot_general(
            cots[f, 96:480], weight[3456:3584], (((1,), (1,)), ((), ())), preferred_element_type=f32
        )
        value = (back[f] - mean_grad - standard_of(f + 2) * mean_cross) * inv + shortcut
        grad_buf[f] = value.astype(bf16)
        grad_copy(f).start()
        return carry

    lax.fori_loop(0, 4, grad_frame, 0)

    each_ctx(lambda peer: sums_copy(sums, sums_in, s_send, s_recv, peer).wait_send())
    each_ctx(lambda peer: sums_copy(sums2, sums2_in, s2_send, s2_recv, peer).wait_send())

    @pl.when(ctx < n_ctx - 1)
    def _():
        clip_halo.wait_send()

    @pl.when(ctx > 0)
    def _():
        edge_halo.wait_send()

    for chunk in range(3):
        pair_copy(chunk).wait_send()
    for quarter in range(4):
        for kind in (Y_FIRST, X_FIRST):
            for k in range(1, 4):
                first_step(quarter, kind, k).wait_send()
                second_step(quarter, kind, k).wait_send()
    for f in range(4):
        out_copy(f).wait()
        grad_copy(f).wait()
    for quarter in range(4):
        for to_lo in range(2):
            for to_core in range(2):
                mine = (z_hi == quarter) & (z_lo == to_lo) & (core == to_core)

                @pl.when(jnp.logical_not(mine))
                def _():
                    third_step(quarter, to_lo, to_core).wait_send()

    place = (z_hi * 2 + z_lo) * 2 + core
    for k in range(1, 16):
        source = (place + k) % 16
        third_arrival(source // 2, source % 2).wait_recv()

    halves = []
    for h in range(2):
        value = step3_in[0, h].astype(f32)
        for from_z in range(1, 8):
            value = value + step3_in[from_z, h].astype(f32)
        halves.append(value)
    value = jnp.concatenate(halves, axis=0) * (1.0 / (4 * n_ctx * n_dp))
    conv_buf[...] = value[:, 0:108]
    short_buf[...] = value.T[108:112]
    ends = [
        pltpu.make_async_copy(conv_buf, conv_grad, out_sem.at[8]),
        pltpu.make_async_copy(short_buf, short_grad, out_sem.at[9]),
    ]
    for copy in ends:
        copy.start()
    for copy in ends:
        copy.wait()


def store(*refs):
    sources, targets, sems = refs[0:4], refs[4:8], refs[8]
    pairs = [(sources[k].at[f], targets[k].at[f]) for k in range(2) for f in range(4)]
    pairs += [(sources[k], targets[k]) for k in range(2, 4)]
    copies = [pltpu.make_async_copy(source, target, sems.at[k]) for k, (source, target) in enumerate(pairs)]
    for copy in copies:
        copy.start()
    for copy in copies:
        copy.wait()


def body(n_dp, n_ctx, clip_in, norm_gain, norm_bias, conv_weight, short_weight, out_cotangent):
    f32, bf16 = jnp.float32, jnp.bfloat16
    anywhere = pl.BlockSpec(memory_space=pl.ANY)
    hbm = pl.BlockSpec(memory_space=pltpu.HBM)
    dma = pltpu.SemaphoreType.DMA
    shapes = (
        jax.ShapeDtypeStruct((4, 384, 256), bf16),
        jax.ShapeDtypeStruct((4, 384, 128), bf16),
        jax.ShapeDtypeStruct((32, 108), f32),
        jax.ShapeDtypeStruct((4, 32), f32),
    )
    results = pl.pallas_call(
        functools.partial(kernel, n_dp, n_ctx),
        out_shape=shapes,
        in_specs=[hbm] * 6,
        out_specs=(anywhere,) * 4,
        scratch_shapes=[
            pltpu.VMEM((6, 384, 128), bf16),
            pltpu.VMEM((4, 576, 256), bf16),
            pltpu.VMEM((1, 128), f32),
            pltpu.VMEM((1, 128), f32),
            pltpu.VMEM((3584, 256), bf16),
            pltpu.VMEM((2304, 384), bf16),
            pltpu.VMEM((6, 576, 384), bf16),
            pltpu.VMEM((4, 384, 128), f32),
            pltpu.VMEM((2, 384, 128), bf16),
            pltpu.VMEM((2, 384, 128), bf16),
            pltpu.VMEM((256, 1536), bf16),
            pltpu.VMEM((2, 128), f32),
            pltpu.VMEM((n_ctx, 2, 128), f32),
            pltpu.VMEM((2, 128), f32),
            pltpu.VMEM((n_ctx, 2, 128), f32),
            pltpu.VMEM((3, n_ctx, 2, 16, 1280), f32),
            pltpu.VMEM((3, n_ctx, 16, 1280), f32),
            pltpu.VMEM((128, 3584), f32),
            pltpu.VMEM((4, 4, 32, 512), bf16),
            pltpu.VMEM((4, 4, 32, 512), bf16),
            pltpu.VMEM((4, 4, 128, 128), bf16),
            pltpu.VMEM((4, 4, 128, 128), bf16),
            pltpu.VMEM((4, 2, 4, 32, 128), f32),
            pltpu.VMEM((4, 2, 4, 32, 128), f32),
            pltpu.VMEM((4, 2, 2, 16, 128), f32),
            pltpu.VMEM((8, 2, 16, 128), f32),
            pltpu.VMEM((4, 384, 256), bf16),
            pltpu.VMEM((4, 384, 128), bf16),
            pltpu.VMEM((32, 108), f32),
            pltpu.VMEM((4, 32), f32),
            dma((7,)), dma((2,)), dma((2,)),
            dma((n_ctx,)), dma((n_ctx,)), dma((n_ctx,)), dma((n_ctx,)),
            dma((3,)), dma((3,)), dma((4, 2, 4)), dma((4, 2, 4)), dma((4, 2, 4)), dma((4, 2, 4)),
            dma((4, 2, 2)), dma((8, 2)), dma((10,)),
        ],
        compiler_params=pltpu.CompilerParams(
            collective_id=0, has_side_effects=True, vmem_limit_bytes=48 << 20
        ),
        name="conv_block",
    )(
        *[pltpu.with_memory_space_constraint(value, pltpu.HBM) for value in (
            clip_in.reshape(4, 384, 128), out_cotangent.reshape(4, 384, 256),
            norm_gain.reshape(1, 128), norm_bias.reshape(1, 128), conv_weight, short_weight,
        )]
    )
    out, grad, conv, short = pl.pallas_call(
        store,
        out_shape=shapes,
        in_specs=[anywhere] * 4,
        out_specs=(anywhere,) * 4,
        scratch_shapes=[dma((10,))],
        name="store",
    )(*[pltpu.with_memory_space_constraint(value, pltpu.VMEM) for value in results])
    return out.reshape(1, 4, 4, 96, 256), grad.reshape(1, 4, 4, 96, 128), conv.T, short


def solution(mesh):
    return jax.shard_map(
        functools.partial(body, mesh.shape["dp"], mesh.shape["ctx"]),
        mesh=mesh,
        in_specs=(
            P("dp", "ctx", None, None, None),
            P(),
            P(),
            P(),
            P(),
            P("dp", "ctx", None, None, None),
        ),
        out_specs=(
            P("dp", "ctx", None, None, None),
            P("dp", "ctx", None, None, None),
            P("dp", "ctx"),
            P("dp", "ctx"),
        ),
        check_vma=False,
    )
```
